32 devices in a mesh: shell: 8 (over z, core), patch: 4 (over y, x).
Axes of the slice: x: 2, y: 2, z: 4, core: 2. Of those that a mesh axis runs over, the one named last changes fastest.
Arguments:
- field_j: float32 [2, 256, 128, 128], P(None, 'shell', 'patch'), may hold values from -1 to 1
Outputs:
- beta_field: float32 [256, 128, 128], P('shell', 'patch')
- u_field: float32 [2, 256, 128, 128], P(None, 'shell', 'patch')
- w_field: float32 [256, 128, 128], P('shell', 'patch')
- h_field: float32 [2, 256, 128, 128], P(None, 'shell', 'patch')
The draws below stay inside these ranges and needn't reach their ends.
All inputs are finite; a program needn't handle non-finite values.
Results may differ from the reference program's by a relative error of at most 0.00002.
Values sent between devices are 32-bit elements; how exact they have to be, the bound alone decides.
A program may use at most 64 MiB of HBM per device.

```python
import math
import jax
import jax.numpy as jnp

NTH = 128
NR = 256
NPH = 128


def block_levels(stream_key, shape, cuts, low, high):
    def one(axis_at, shards_of):
        heights = jax.random.uniform(jax.random.fold_in(jax.random.fold_in(stream_key, 6), axis_at), (shards_of,), jnp.float32, low / len(cuts), high / len(cuts))
        return jnp.repeat(jnp.exp(heights), shape[axis_at] // shards_of).reshape((-1,) + (1,) * (len(shape) - axis_at - 1))

    loudness = one(*cuts[0])
    for cut in cuts[1:]:
        loudness = loudness * one(*cut)
    return loudness


def setup_inputs(seed: int = 0) -> dict:
    streams_of = jax.random.split(jax.random.key(seed), 2)
    return {
        "field_j": jnp.clip(jax.random.uniform(streams_of[0], (2, NR, NPH, NTH), jnp.float32, -1.0, 1.0) * block_levels(streams_of[0], (2, NR, NPH, NTH), ((1, 8), (2, 4)), -0.4, 0.0), -1.0, 1.0),
    }


def theta_diff(values):
    zero_col = jnp.zeros(values.shape[:-1] + (1,), values.dtype)
    forward = jnp.concatenate([values[..., 1:], zero_col], axis=-1)
    backward = jnp.concatenate([zero_col, values[..., :-1]], axis=-1)
    return 0.5 * (forward - backward)

def phi_diff(values):
    return 0.5 * (jnp.roll(values, -1, axis=-2) - jnp.roll(values, 1, axis=-2))

def spin_diff(real_part, imag_part, orient):
    return (theta_diff(real_part) - orient * phi_diff(imag_part), theta_diff(imag_part) + orient * phi_diff(real_part))

def reference(field_j):
    radial_step = 1.0 / math.sqrt(NR)
    field_a = field_j[0]
    field_b = field_j[1]
    beyond = jnp.concatenate([field_j[:, 1:], field_j[:, -1:]], axis=1)
    radial = beyond - field_j
    eth_a, eth_b = spin_diff(field_a, field_b, 1.0)
    source = 0.25 * (0.5 * (radial[0] * radial[0] + radial[1] * radial[1]) - (eth_a * eth_a + eth_b * eth_b))
    beta_field = radial_step * jnp.cumsum(source, axis=0)
    growth = jnp.exp(2.0 * beta_field)
    beta_re = theta_diff(beta_field)
    beta_im = phi_diff(beta_field)
    source_ua = growth * (beta_re - (field_a * beta_re + field_b * beta_im))
    source_ub = growth * (beta_im - (field_b * beta_re - field_a * beta_im))
    u_field = radial_step * jnp.cumsum(jnp.stack([source_ua, source_ub]), axis=1)
    u_a = u_field[0]
    u_b = u_field[1]
    ethu_a, ethu_b = spin_diff(u_a, u_b, 1.0)
    baru_a, baru_b = spin_diff(u_a, u_b, -1.0)
    barj_a, barj_b = spin_diff(field_a, field_b, -1.0)
    source_w = growth * baru_a + (field_b * u_a - field_a * u_b)
    w_field = radial_step * jnp.cumsum(source_w, axis=0)
    source_ha = ethu_a + u_a * barj_a - u_b * barj_b + beta_field * field_a
    source_hb = ethu_b + u_a * barj_b + u_b * barj_a + beta_field * field_b
    h_field = radial_step * jnp.cumsum(jnp.stack([source_ha, source_hb]), axis=1)
    return (beta_field, u_field, w_field, h_field)
```

```python
import functools
import math

import jax
import jax.numpy as jnp
from jax import lax
from jax.experimental import pallas as pl
from jax.experimental.pallas import tpu as pltpu
from jax.sharding import PartitionSpec as P

PAD = 8
LAP = 4


def remote(src, dst, send_sem, recv_sem, shell, patch):
    return pltpu.make_async_remote_copy(
        src_ref=src,
        dst_ref=dst,
        send_sem=send_sem,
        recv_sem=recv_sem,
        device_id=(shell, patch),
        device_id_type=pl.DeviceIdType.MESH,
    )


def make_theta(lanes):
    lane = lax.broadcasted_iota(jnp.int32, (8, lanes), 1)
    keep_f = jnp.where(lane == lanes - 1, 0.0, 0.5).astype(jnp.float32)
    keep_b = jnp.where(lane == 0, 0.0, 0.5).astype(jnp.float32)

    def theta(x):
        reps = x.shape[0] // 8
        mf = jnp.concatenate([keep_f] * reps, axis=0) if reps > 1 else keep_f
        mb = jnp.concatenate([keep_b] * reps, axis=0) if reps > 1 else keep_b
        return pltpu.roll(x, lanes - 1, 1) * mf - pltpu.roll(x, 1, 1) * mb

    return theta


def kernel(shells, patches, step, j_hbm, jp, up, bfin, gs, barj, cw, ch, pre,
           bp, es, dr, jnext, jedge, jhalo, bedge, bhalo,
           sum_b, slot_b, slot_l, slot_r, bt, su, seg_e, seg_l, slot_e, slot_s, acc, fsrc, fslot,
           load_sem, rad_sem, jh_send, jh_recv, bh_send, bh_recv,
           b_send, b_recv, e_send, e_recv, s_send, s_recv, f_sem):
    radii, cols, lanes = jp.shape[1], jp.shape[2] - 2 * PAD, jp.shape[3]
    chips = shells // 2
    half = cols // 2
    wide = half + 2 * LAP
    tall = cols + 8
    f32 = jnp.float32
    shell, patch = lax.axis_index("shell"), lax.axis_index("patch")
    chip, core = shell // 2, shell % 2
    partner = shell + 1 - 2 * core
    right = lax.rem(patch + 1, patches)
    left = lax.rem(patch + patches - 1, patches)
    inner = slice(PAD, PAD + cols)
    above = slice(PAD + 1, PAD + cols + 1)
    below = slice(PAD - 1, PAD + cols - 1)
    before, after = slice(PAD - 1, PAD), slice(PAD + cols, PAD + cols + 1)
    theta = make_theta(lanes)

    load = pltpu.make_async_copy(j_hbm, jp.at[:, :, pl.ds(PAD, cols), :], load_sem)
    load.start()
    barrier = pltpu.get_barrier_semaphore()
    for d in range(shells):
        there = lax.rem(shell + d, shells)
        for p in (patch, left, right):
            if d == 0 and p is patch:
                continue
            pl.semaphore_signal(barrier, inc=1, device_id=(there, p),
                                device_id_type=pl.DeviceIdType.MESH)

    def halo(edge, got, send, recv):
        to_left = remote(edge.at[0], got.at[1], send.at[0], recv.at[1], shell, left)
        to_right = remote(edge.at[1], got.at[0], send.at[1], recv.at[0], shell, right)
        return to_left, to_right

    load.wait()

    def pack(k, c):
        for f in range(2):
            jedge[0, f, pl.ds(k, 1), :] = jp[f, k, PAD:PAD + 1, :]
            jedge[1, f, pl.ds(k, 1), :] = jp[f, k, PAD + cols - 1:PAD + cols, :]
        return c

    lax.fori_loop(0, radii, pack, 0, unroll=8)
    pl.semaphore_wait(barrier, 3 * shells - 1)

    j_left, j_right = halo(jedge, jhalo, jh_send, jh_recv)
    j_left.start()
    j_right.start()

    @pl.when(shell > 0)
    def _():
        remote(j_hbm.at[:, 0], jnext, rad_sem.at[0], rad_sem.at[1], shell - 1, patch).start()

    def beta_step(k, next_of, spans, totals):
        new = []
        for (lo, n), total in zip(spans, totals):
            at = slice(PAD + lo, PAD + lo + n)
            up1 = slice(PAD + lo + 1, PAD + lo + n + 1)
            dn1 = slice(PAD + lo - 1, PAD + lo + n - 1)
            a, b = jp[0, k, at], jp[1, k, at]
            ra, rb = next_of(0, k, lo, n) - a, next_of(1, k, lo, n) - b
            ta, tb = theta(a), theta(b)
            pa = 0.5 * (jp[0, k, up1] - jp[0, k, dn1])
            pb = 0.5 * (jp[1, k, up1] - jp[1, k, dn1])
            ea, eb = ta - pb, tb + pa
            barj[0, k, lo:lo + n] = ta + pb
            barj[1, k, lo:lo + n] = tb - pa
            total = total + 0.25 * (0.5 * (ra * ra + rb * rb) - (ea * ea + eb * eb))
            bp[k, at] = total
            if lo == 0:
                bedge[0, 0, pl.ds(k, 1), :] = total[:1]
                bedge[0, 1, pl.ds(k, 1), :] = total[1:2]
            if lo + n == cols:
                bedge[1, 0, pl.ds(k, 1), :] = total[n - 2:n - 1]
                bedge[1, 1, pl.ds(k, 1), :] = total[n - 1:]
            new.append(total)
        return tuple(new)

    def from_jp(f, k, lo, n):
        return jp[f, k + 1, PAD + lo:PAD + lo + n]

    def from_next(f, k, lo, n):
        return jnext[f, lo:lo + n]

    def beta_span(spans, middle):
        zeros = tuple(jnp.zeros((n, lanes), f32) for _, n in spans)
        totals = lax.fori_loop(0, radii - 1, lambda k, t: beta_step(k, from_jp, spans, t), zeros, unroll=2)
        middle()
        totals = beta_step(radii - 1, from_next, spans, totals)
        for (lo, n), total in zip(spans, totals):
            sum_b[lo:lo + n] = total

    def wait_next():
        @pl.when(shell == shells - 1)
        def _():
            for f in range(2):
                jnext[f] = jp[f, radii - 1, inner]

        @pl.when(shell < shells - 1)
        def _():
            remote(j_hbm.at[:, 0], jnext, rad_sem.at[0], rad_sem.at[1], shell, patch).wait_recv()

    beta_span(((8, cols - 16),), wait_next)
    j_left.wait_recv()
    j_right.wait_recv()

    def unpack(k, c):
        for f in range(2):
            jp[f, k, before, :] = jhalo[0, f, pl.ds(k, 1), :]
            jp[f, k, after, :] = jhalo[1, f, pl.ds(k, 1), :]
        return c

    lax.fori_loop(0, radii, unpack, 0, unroll=8)
    beta_span(((0, 8), (cols - 8, 8)), lambda: None)

    def b_copies(d):
        there = shell + d
        return [
            remote(sum_b, slot_b.at[d - 1], b_send.at[0, d - 1], b_recv.at[0, d - 1], there, patch),
            remote(sum_b.at[pl.ds(cols - 8, 8)], slot_l.at[d - 1], b_send.at[1, d - 1], b_recv.at[1, d - 1],
                   there, right),
            remote(sum_b.at[pl.ds(0, 8)], slot_r.at[d - 1], b_send.at[2, d - 1], b_recv.at[2, d - 1],
                   there, left),
        ]

    b_left, b_right = halo(bedge, bhalo, bh_send, bh_recv)
    for d in range(1, shells):
        @pl.when(shell + d < shells)
        def _():
            for copy in b_copies(d):
                copy.start()
        if d == 1:
            b_left.start()
            b_right.start()

    zero = jnp.zeros((cols, lanes), f32)

    def local_step(k, carry):
        se, sa, sb, sja, sjb, sba, sbb = carry
        beta = bp[k, inner]
        grow = jnp.exp((2.0 * step) * beta)
        es[k, inner] = grow
        dr[k, inner] = theta(beta)
        a, b = jp[0, k, inner], jp[1, k, inner]
        return (se + grow, sa + a, sb + b, sja + barj[0, k], sjb + barj[1, k], sba + beta * a, sbb + beta * b)

    se, sa, sb, sja, sjb, sba, sbb = lax.fori_loop(0, radii, local_step, (zero,) * 7, unroll=2)
    for c in range(2):
        rows = slice(c * half, (c + 1) * half)
        for i, x in enumerate((sa, sb, sja, sjb)):
            seg_e[c, i * half:(i + 1) * half] = x[rows]

    def seg_copies(dz, seg, slot, send, recv):
        return [remote(seg.at[e], slot.at[(dz - 1) * 2 + core], send.at[(dz - 1) * 2 + e],
                       recv.at[(dz - 1) * 2 + core], (chip + dz) * 2 + e, patch) for e in range(2)]

    def own_copy(seg, slot, send, recv):
        last = 2 * (chips - 1)
        return remote(seg.at[1], slot.at[last], send.at[last], recv.at[last], partner, patch)

    def start_seg(seg, slot, send, recv):
        @pl.when(core == 0)
        def _():
            own_copy(seg, slot, send, recv).start()

        for dz in range(chips - 1, 0, -1):
            @pl.when(chip + dz < chips)
            def _():
                for copy in seg_copies(dz, seg, slot, send, recv):
                    copy.start()

    start_seg(seg_e, slot_e, e_send, e_recv)

    b_left.wait_recv()
    b_right.wait_recv()

    def halo_step(k, c):
        bp[k, PAD - 2:PAD - 1, :] = bhalo[0, 0, pl.ds(k, 1), :]
        bp[k, PAD - 1:PAD, :] = bhalo[0, 1, pl.ds(k, 1), :]
        bp[k, PAD + cols:PAD + cols + 1, :] = bhalo[1, 0, pl.ds(k, 1), :]
        bp[k, PAD + cols + 1:PAD + cols + 2, :] = bhalo[1, 1, pl.ds(k, 1), :]
        return c

    lax.fori_loop(0, radii, halo_step, 0, unroll=8)

    def halo_exp(k, c):
        for lo in (0, PAD + cols):
            x = bp[k, lo:lo + 8]
            es[k, lo:lo + 8] = jnp.exp((2.0 * step) * x)
            dr[k, lo:lo + 8] = theta(x)
        return c

    lax.fori_loop(0, radii, halo_exp, 0, unroll=4)

    bt[...] = jnp.zeros_like(bt)
    for d in range(1, shells):
        @pl.when(shell >= d)
        def _():
            for i, slot in enumerate((slot_b, slot_l, slot_r)):
                src = (sum_b, sum_b.at[pl.ds(0, 8)], sum_b.at[pl.ds(0, 8)])[i]
                remote(src, slot.at[d - 1], b_send.at[i, d - 1], b_recv.at[i, d - 1], shell, patch).wait_recv()
            bt[inner] += slot_b[d - 1]
            bt[0:PAD] += slot_l[d - 1]
            bt[PAD + cols:] += slot_r[d - 1]

    first = PAD - 1
    mid, hi, lo = slice(first, first + tall), slice(first + 1, first + tall + 1), slice(first - 1, first + tall - 1)
    base_r = theta(bt[mid])
    base_i = bt[hi] - bt[lo]
    base_g = step * jnp.exp((2.0 * step) * bt[mid])
    wide_zero = jnp.zeros((tall, lanes), f32)

    def u_step(k, carry):
        sa, sb = carry
        growth = base_g * es[k, mid]
        br = dr[k, mid] + base_r
        bi = 0.5 * ((bp[k, hi] - bp[k, lo]) + base_i)
        a, b = jp[0, k, mid], jp[1, k, mid]
        sa = sa + growth * (br - (a * br + b * bi))
        sb = sb + growth * (bi - (b * br - a * bi))
        up[0, k, mid] = sa
        up[1, k, mid] = sb
        return sa, sb

    ua_sum, ub_sum = lax.fori_loop(0, radii, u_step, (wide_zero, wide_zero), unroll=2)
    su[0, mid] = ua_sum
    su[1, mid] = ub_sum

    def sums_step(k, carry):
        w1, w2, q, qa, ub_all, ha, hb = carry
        a, b = jp[0, k, inner], jp[1, k, inner]
        ua, ub = up[0, k, inner], up[1, k, inner]
        ta = theta(ua)
        pb = 0.5 * (up[1, k, above] - up[1, k, below])
        ja, jb = barj[0, k], barj[1, k]
        w1 = w1 + es[k, inner] * (ta + pb)
        w2 = w2 + (b * ua - a * ub)
        q = q + (ta - pb)
        qa = qa + (up[0, k, above] - up[0, k, below])
        ub_all = ub_all + ub
        ha = ha + (ua * ja - ub * jb)
        hb = hb + (ua * jb + ub * ja)
        return w1, w2, q, qa, ub_all, ha, hb

    w1, w2, q, qa, ub_all, ha, hb = lax.fori_loop(0, radii, sums_step, (zero,) * 7, unroll=2)
    full_b = bt[inner]
    grow_b = jnp.exp((2.0 * step) * full_b)
    planes = (grow_b * se, grow_b * w1 + w2, q + ha + (sba + full_b * sa),
              theta(ub_all) + 0.5 * qa + hb + (sbb + full_b * sb))
    for c in range(2):
        for f in range(2):
            start = PAD + c * half - LAP
            seg_l[c, f * wide:(f + 1) * wide] = su[f, start:start + wide]
        for i, x in enumerate(planes):
            at = 2 * wide + i * half
            seg_l[c, at:at + half] = x[c * half:(c + 1) * half]

    start_seg(seg_l, slot_s, s_send, s_recv)

    def wh_step(k, carry):
        sw, sa, sb = carry
        beta = bp[k, inner] + full_b
        bfin[k] = step * beta
        growth = grow_b * es[k, inner]
        gs[k] = growth
        a, b = jp[0, k, inner], jp[1, k, inner]
        ua, ub = up[0, k, inner], up[1, k, inner]
        ta, tb = theta(ua), theta(ub)
        pa = 0.5 * (up[0, k, above] - up[0, k, below])
        pb = 0.5 * (up[1, k, above] - up[1, k, below])
        ja, jb = barj[0, k], barj[1, k]
        sw = sw + (growth * (ta + pb) + (b * ua - a * ub))
        sa = sa + ((ta - pb) + ua * ja - ub * jb + beta * a)
        sb = sb + ((tb + pa) + ua * jb + ub * ja + beta * b)
        cw[k] = sw
        ch[0, k] = sa
        ch[1, k] = sb
        return sw, sa, sb

    lax.fori_loop(0, radii, wh_step, (zero, zero, zero))

    parts = [slice(2 * wide + i * half, 2 * wide + (i + 1) * half) for i in range(4)]
    w_at, ha_at, hb_at = parts[:3]
    own, over, under = slice(LAP, LAP + half), slice(LAP + 1, LAP + half + 1), slice(LAP - 1, LAP + half - 1)

    def at_b(s):
        return slice(s.start + wide, s.stop + wide)

    def compose(e, s):
        ca, cb = acc[own], acc[at_b(own)]
        ta, tb = theta(ca), theta(cb)
        pa = 0.5 * (acc[over] - acc[under])
        pb = 0.5 * (acc[at_b(over)] - acc[at_b(under)])
        a, b, ja, jb = (e[i * half:(i + 1) * half] for i in range(4))
        g, w, ha, hb = (s[p] for p in parts)
        n = float(radii)
        acc[w_at] += w + g * (ta + pb) + (b * ca - a * cb)
        acc[ha_at] += ha + n * (ta - pb) + (ca * ja - cb * jb)
        acc[hb_at] += hb + n * (tb + pa) + (ca * jb + cb * ja)
        acc[0:2 * wide] += s[0:2 * wide]

    def wait_seg(i):
        remote(seg_e.at[0], slot_e.at[i], e_send.at[i], e_recv.at[i], shell, patch).wait_recv()
        remote(seg_l.at[0], slot_s.at[i], s_send.at[i], s_recv.at[i], shell, patch).wait_recv()

    acc[...] = jnp.zeros_like(acc)
    for dz in range(chips - 1, 0, -1):
        @pl.when(chip >= dz)
        def _():
            for e in range(2):
                i = (dz - 1) * 2 + e
                wait_seg(i)
                compose(slot_e.at[i], slot_s.at[i])

    forward = remote(fsrc, fslot, f_sem.at[0], f_sem.at[1], partner, patch)

    @pl.when(core == 0)
    def _():
        pre[0] = acc[...]
        compose(seg_e.at[0], seg_l.at[0])
        fsrc[...] = acc[...]
        forward.start()
        forward.wait_recv()
        pre[1] = fslot[...]

    @pl.when(core == 1)
    def _():
        fsrc[...] = acc[...]
        forward.start()
        last = 2 * (chips - 1)
        wait_seg(last)
        compose(slot_e.at[last], slot_s.at[last])
        pre[1] = acc[...]
        forward.wait_recv()
        pre[0] = fslot[...]

    for copy in (j_left, j_right, b_left, b_right, forward):
        copy.wait_send()

    @pl.when(shell > 0)
    def _():
        remote(j_hbm.at[:, 0], jnext, rad_sem.at[0], rad_sem.at[1], shell - 1, patch).wait_send()

    for d in range(1, shells):
        @pl.when(shell + d < shells)
        def _():
            for copy in b_copies(d):
                copy.wait_send()

    for group in ((seg_e, slot_e, e_send, e_recv), (seg_l, slot_s, s_send, s_recv)):
        @pl.when(core == 0)
        def _():
            own_copy(*group).wait_send()

        for dz in range(1, chips):
            @pl.when(chip + dz < chips)
            def _():
                for copy in seg_copies(dz, *group):
                    copy.wait_send()


def tail(step, jp, up, bfin, gs, barj, cw, ch, pre, beta_out, u_out, w_out, h_out, uv, wv, hv, sems):
    radii, cols, lanes = cw.shape
    half = cols // 2
    wide = half + 2 * LAP
    inner = slice(PAD, PAD + cols)
    theta = make_theta(lanes)
    copies = [pltpu.make_async_copy(bfin, beta_out, sems.at[0, 0])]
    copies[0].start()

    def rows(at, n):
        return jnp.concatenate([pre[0, at:at + n], pre[1, at:at + n]], axis=0)

    ca, cb = rows(LAP, half), rows(wide + LAP, half)
    ta, tb = theta(ca), theta(cb)
    pa = 0.5 * (rows(LAP + 1, half) - rows(LAP - 1, half))
    pb = 0.5 * (rows(wide + LAP + 1, half) - rows(wide + LAP - 1, half))
    re_bar, eth_a, eth_b = ta + pb, ta - pb, tb + pa
    sq = step * step

    def final(k, carry):
        dw, da, db = carry
        a, b = jp[0, k, inner], jp[1, k, inner]
        ja, jb = barj[0, k], barj[1, k]
        dw = dw + (gs[k] * re_bar + (b * ca - a * cb))
        da = da + (eth_a + (ca * ja - cb * jb))
        db = db + (eth_b + (ca * jb + cb * ja))
        uv[0, k] = step * (up[0, k, inner] + ca)
        uv[1, k] = step * (up[1, k, inner] + cb)
        wv[k] = sq * (cw[k] + dw)
        hv[0, k] = sq * (ch[0, k] + da)
        hv[1, k] = sq * (ch[1, k] + db)
        return dw, da, db

    carry = tuple(rows(2 * wide + i * half, half) for i in range(3))
    chunks = sems.shape[1]
    size = radii // chunks
    for i in range(chunks):
        carry = lax.fori_loop(i * size, (i + 1) * size, final, carry, unroll=2)
        at = pl.ds(i * size, size)
        more = [pltpu.make_async_copy(uv.at[:, at], u_out.at[:, at], sems.at[1, i]),
                pltpu.make_async_copy(wv.at[at], w_out.at[at], sems.at[2, i]),
                pltpu.make_async_copy(hv.at[:, at], h_out.at[:, at], sems.at[3, i])]
        for copy in more:
            copy.start()
        copies += more
    for copy in copies:
        copy.wait()


def solution(mesh):
    shells, patches = mesh.shape["shell"], mesh.shape["patch"]
    chips = shells // 2

    def local(field_j):
        _, radii, cols, lanes = field_j.shape
        step = 1.0 / math.sqrt(radii * shells)
        f32 = jnp.float32
        vm = lambda *s: pltpu.VMEM(s, f32)
        tall = cols + 2 * PAD
        half = cols // 2
        wide = half + 2 * LAP
        late, early, state = 2 * wide + 4 * half, 4 * half, 2 * wide + 3 * half
        segs = 2 * (chips - 1) + 1
        outer = shells - 1
        dma = pltpu.SemaphoreType.DMA
        scratch = [
            vm(radii, tall, lanes), vm(radii, tall, lanes), vm(radii, tall, lanes), vm(2, cols, lanes),
            vm(2, 2, radii, lanes), vm(2, 2, radii, lanes), vm(2, 2, radii, lanes), vm(2, 2, radii, lanes),
            vm(cols, lanes), vm(outer, cols, lanes), vm(outer, 8, lanes), vm(outer, 8, lanes),
            vm(tall, lanes), vm(2, tall, lanes),
            vm(2, early, lanes), vm(2, late, lanes), vm(segs, early, lanes), vm(segs, late, lanes),
            vm(state, lanes), vm(state, lanes), vm(state, lanes),
            dma, dma((2,)), dma((2,)), dma((2,)), dma((2,)), dma((2,)),
            dma((3, outer)), dma((3, outer)), dma((segs,)), dma((segs,)), dma((segs,)), dma((segs,)), dma((2,)),
        ]
        shape = lambda *s: jax.ShapeDtypeStruct(s, f32)
        vmem = pl.BlockSpec(memory_space=pltpu.VMEM)
        hbm = pl.BlockSpec(memory_space=pltpu.HBM)
        plain, pair = (radii, cols, lanes), (2, radii, cols, lanes)
        padded = (2, radii, tall, lanes)
        found = pl.pallas_call(
            functools.partial(kernel, shells, patches, step),
            out_shape=(shape(*padded), shape(*padded), shape(*plain), shape(*plain), shape(*pair),
                       shape(*plain), shape(*pair), shape(2, state, lanes)),
            in_specs=[hbm],
            out_specs=(vmem,) * 8,
            scratch_shapes=scratch,
            compiler_params=pltpu.CompilerParams(
                collective_id=0, has_side_effects=True, vmem_limit_bytes=28 * 1024 * 1024),
        )(pltpu.with_memory_space_constraint(field_j, pltpu.HBM))
        return pl.pallas_call(
            functools.partial(tail, step),
            out_shape=(shape(*plain), shape(*pair), shape(*plain), shape(*pair)),
            in_specs=[vmem] * 8,
            out_specs=(hbm,) * 4,
            scratch_shapes=[vm(*pair), vm(*plain), vm(*pair), dma((4, 4))],
            compiler_params=pltpu.CompilerParams(vmem_limit_bytes=28 * 1024 * 1024),
        )(*found)

    return jax.shard_map(
        local,
        mesh=mesh,
        in_specs=(P(None, "shell", "patch", None),),
        out_specs=(
            P("shell", "patch", None),
            P(None, "shell", "patch", None),
            P("shell", "patch", None),
            P(None, "shell", "patch", None),
        ),
        check_vma=False,
    )
```

```python
import functools
import math

import jax
import jax.numpy as jnp
from jax import lax
from jax.experimental import pallas as pl
from jax.experimental.pallas import tpu as pltpu
from jax.sharding import PartitionSpec as P

PAD = 8


def remote(src, dst, send_sem, recv_sem, shell, patch):
    return pltpu.make_async_remote_copy(
        src_ref=src,
        dst_ref=dst,
        send_sem=send_sem,
        recv_sem=recv_sem,
        device_id=(shell, patch),
        device_id_type=pl.DeviceIdType.MESH,
    )


def make_theta(lanes):
    lane = lax.broadcasted_iota(jnp.int32, (8, lanes), 1)
    keep_f = jnp.where(lane == lanes - 1, 0.0, 0.5).astype(jnp.float32)
    keep_b = jnp.where(lane == 0, 0.0, 0.5).astype(jnp.float32)

    def theta(x):
        reps = x.shape[0] // 8
        mf = jnp.concatenate([keep_f] * reps, axis=0) if reps > 1 else keep_f
        mb = jnp.concatenate([keep_b] * reps, axis=0) if reps > 1 else keep_b
        return pltpu.roll(x, lanes - 1, 1) * mf - pltpu.roll(x, 1, 1) * mb

    return theta


def whole(edges, middle, f, k):
    return jnp.concatenate([edges[0, f, k], middle[f, k], edges[1, f, k]], axis=0)


def eth_planes(theta, pair, inner, above, below):
    ta, tb = theta(pair[0, inner]), theta(pair[1, inner])
    pa = 0.5 * (pair[0, above] - pair[0, below])
    pb = 0.5 * (pair[1, above] - pair[1, below])
    return ta + pb, ta - pb, tb + pa


def beta_point(theta, jp, k, lo, n, next_a, next_b):
    at = slice(PAD + lo, PAD + lo + n)
    up1 = slice(PAD + lo + 1, PAD + lo + n + 1)
    dn1 = slice(PAD + lo - 1, PAD + lo + n - 1)
    a, b = jp[0, k, at], jp[1, k, at]
    ra, rb = next_a - a, next_b - b
    ta, tb = theta(a), theta(b)
    pa = 0.5 * (jp[0, k, up1] - jp[0, k, dn1])
    pb = 0.5 * (jp[1, k, up1] - jp[1, k, dn1])
    ea, eb = ta - pb, tb + pa
    return 0.25 * (0.5 * (ra * ra + rb * rb) - (ea * ea + eb * eb)), ta + pb, tb - pa


def gather(shells, patches, j_hbm, jp, jnext, b_in, barj_in, jnear, jedge, jhalo, load_sem, rad_sem, jh_send, jh_recv):
    radii, cols, lanes = jp.shape[1], jp.shape[2] - 2 * PAD, jp.shape[3]
    shell, patch = lax.axis_index("shell"), lax.axis_index("patch")
    right = lax.rem(patch + 1, patches)
    left = lax.rem(patch + patches - 1, patches)
    inner = slice(PAD, PAD + cols)
    before, after = slice(PAD - 1, PAD), slice(PAD + cols, PAD + cols + 1)
    theta = make_theta(lanes)

    load = pltpu.make_async_copy(j_hbm, jp.at[:, :, pl.ds(PAD, cols), :], load_sem)
    load.start()
    barrier = pltpu.get_barrier_semaphore()
    for p in (left, right):
        pl.semaphore_signal(barrier, inc=1, device_id=(shell, p), device_id_type=pl.DeviceIdType.MESH)

    @pl.when(shell > 0)
    def _():
        pl.semaphore_signal(barrier, inc=1, device_id=(shell - 1, patch), device_id_type=pl.DeviceIdType.MESH)

    @pl.when(shell < shells - 1)
    def _():
        pl.semaphore_signal(barrier, inc=1, device_id=(shell + 1, patch), device_id_type=pl.DeviceIdType.MESH)

    load.wait()

    def pack(k, c):
        for f in range(2):
            jedge[0, f, pl.ds(k, 1), :] = jp[f, k, PAD:PAD + 1, :]
            jedge[1, f, pl.ds(k, 1), :] = jp[f, k, PAD + cols - 1:PAD + cols, :]
        return c

    lax.fori_loop(0, radii, pack, 0, unroll=8)
    pl.semaphore_wait(barrier, 2 + (shell > 0).astype(jnp.int32) + (shell < shells - 1).astype(jnp.int32))
    to_left = remote(jedge.at[0], jhalo.at[1], jh_send.at[0], jh_recv.at[1], shell, left)
    to_right = remote(jedge.at[1], jhalo.at[0], jh_send.at[1], jh_recv.at[0], shell, right)
    to_left.start()
    to_right.start()

    def down(there):
        return remote(j_hbm.at[:, 0], jnear, rad_sem.at[0], rad_sem.at[1], there, patch)

    @pl.when(shell > 0)
    def _():
        down(shell - 1).start()

    lo, n = 8, cols - 16

    def keep(k, found, total):
        source, ja, jb = found
        barj_in[0, k], barj_in[1, k] = ja, jb
        b_in[k] = total + source
        return total + source

    def beta_step(k, total):
        at = slice(PAD + lo, PAD + lo + n)
        return keep(k, beta_point(theta, jp, k, lo, n, jp[0, k + 1, at], jp[1, k + 1, at]), total)

    total = lax.fori_loop(0, radii - 1, beta_step, jnp.zeros((n, lanes), jnp.float32), unroll=2)

    @pl.when(shell == shells - 1)
    def _():
        for f in range(2):
            jnext[f] = jp[f, radii - 1, inner]

    @pl.when(shell < shells - 1)
    def _():
        down(shell).wait_recv()
        jnext[...] = jnear[...]

    keep(radii - 1, beta_point(theta, jp, radii - 1, lo, n, jnext[0, lo:lo + n], jnext[1, lo:lo + n]), total)
    to_left.wait_recv()
    to_right.wait_recv()

    def unpack(k, c):
        for f in range(2):
            jp[f, k, before, :] = jhalo[0, f, pl.ds(k, 1), :]
            jp[f, k, after, :] = jhalo[1, f, pl.ds(k, 1), :]
        return c

    lax.fori_loop(0, radii, unpack, 0, unroll=8)
    to_left.wait_send()
    to_right.wait_send()

    @pl.when(shell > 0)
    def _():
        down(shell - 1).wait_send()


def kernel(shells, patches, step, jp, jnext, b_in, barj_in, up, bfin, gs, cw, ch, ct, below_h, barj_e,
           bp, es, dr, bt, bedge, bhalo, below_b, below_u,
           sum_b, part_b, tot_b, slot_b, pre_b,
           sum_u, part_u, tot_u, slot_u, pre_u,
           sum_h, part_h, tot_h, slot_h, pre_h,
           rim_b, rtot_b, rpart_b, rslot_b, rim_u, rtot_u, rpart_u, rslot_u,
           edge_send, edge_recv, part_sem, send_sem, recv_sem, fwd_sem,
           rpart_send, rpart_recv, rim_send, rim_recv):
    radii, cols, lanes = cw.shape
    tall = cols + 8
    f32 = jnp.float32
    chips = shells // 2
    shell, patch = lax.axis_index("shell"), lax.axis_index("patch")
    chip, core = shell // 2, shell % 2
    partner = shell + 1 - 2 * core
    right = lax.rem(patch + 1, patches)
    left = lax.rem(patch + patches - 1, patches)
    inner = slice(PAD, PAD + cols)
    above = slice(PAD + 1, PAD + cols + 1)
    below = slice(PAD - 1, PAD + cols - 1)
    theta = make_theta(lanes)

    barrier = pltpu.get_barrier_semaphore()
    for d in range(shells):
        there = lax.rem(shell + d, shells)
        for p in (patch, left, right):
            if d == 0 and p is patch:
                continue
            pl.semaphore_signal(barrier, inc=1, device_id=(there, p),
                                device_id_type=pl.DeviceIdType.MESH)

    spans = ((0, 0), (1, cols - 8))

    def edge_step(k, next_of, totals):
        new = []
        for (side, lo), total in zip(spans, totals):
            source, ja, jb = beta_point(theta, jp, k, lo, 8, next_of(0, k, lo), next_of(1, k, lo))
            barj_e[side, 0, k], barj_e[side, 1, k] = ja, jb
            total = total + source
            bp[k, PAD + lo:PAD + lo + 8] = total
            at = 6 * side
            bedge[side, 0, pl.ds(k, 1), :] = total[at:at + 1]
            bedge[side, 1, pl.ds(k, 1), :] = total[at + 1:at + 2]
            new.append(total)
        return tuple(new)

    zero8 = jnp.zeros((8, lanes), f32)
    totals = lax.fori_loop(
        0, radii - 1, lambda k, t: edge_step(k, lambda f, k, lo: jp[f, k + 1, PAD + lo:PAD + lo + 8], t),
        (zero8, zero8), unroll=2)
    totals = edge_step(radii - 1, lambda f, k, lo: jnext[f, lo:lo + 8], totals)
    sum_b[0:8] = totals[0]
    sum_b[8:cols - 8] = b_in[radii - 1]
    sum_b[cols - 8:] = totals[1]

    def pieces(stage, own, part, tot, slots, both):
        half = own.shape[0] // 2
        mine = pl.ds(pl.multiple_of(core * half, 8), half)
        first = remote(own, part, part_sem.at[stage, 0], part_sem.at[stage, 1], partner, patch)
        sends = []
        for d in range(1, chips):
            if both:
                sends.append([
                    remote(tot.at[mine], slots.at[d - 1, mine], send_sem.at[stage, d - 1, e],
                           recv_sem.at[stage, d - 1, core], (chip + d) * 2 + e, patch)
                    for e in range(2)])
            else:
                sends.append([
                    remote(tot.at[mine], slots.at[d - 1, mine], send_sem.at[stage, d - 1, 0],
                           recv_sem.at[stage, d - 1, 0], (chip + d) * 2 + core, patch)])
        return mine, half, first, sends

    def rim_pieces(stage, rim, rtot, rpart, rslot):
        over = left * (1 - core) + right * core
        near = [
            remote(rim.at[0], rpart.at[1], rpart_send.at[stage, 0], rpart_recv.at[stage, 1], partner, left),
            remote(rim.at[1], rpart.at[0], rpart_send.at[stage, 1], rpart_recv.at[stage, 0], partner, right)]
        far = [[
            remote(rtot.at[core], rslot.at[d - 1, 1 - core], rim_send.at[stage, d - 1, e],
                   rim_recv.at[stage, d - 1, 1 - core], (chip + d) * 2 + e, over)
            for e in range(2)] for d in range(1, chips)]
        return near, far

    def begin(stage, own, part, tot, slots, both, rims=None, lines=None):
        mine, half, first, sends = pieces(stage, own, part, tot, slots, both)
        first.start()
        if rims is not None:
            rim, rtot, rpart, rslot = rims
            for side in range(2):
                for i, r in enumerate(lines[side]):
                    rim[side, i:i + 1] = own[r:r + 1]
            near, far = rim_pieces(stage, rim, rtot, rpart, rslot)

            @pl.when(core == 0)
            def _():
                for copy in near:
                    copy.start()

        first.wait_recv()
        tot[mine] = own[mine] + part[mine]
        if rims is not None:
            for side in range(2):
                for i, r in enumerate(lines[side]):
                    rtot[side, i:i + 1] = own[r:r + 1] + part[r:r + 1]
        for d in range(1, chips):
            @pl.when(chip + d < chips)
            def _():
                for copy in sends[d - 1]:
                    copy.start()
                if rims is not None:
                    for copy in far[d - 1]:
                        copy.start()

    def end(stage, own, part, tot, slots, pre, out, both, rims=None):
        mine, half, first, sends = pieces(stage, own, part, tot, slots, both)
        if rims is not None:
            rim, rtot, rpart, rslot = rims
            near, far = rim_pieces(stage, rim, rtot, rpart, rslot)

        @pl.when(core == 0)
        def _():
            out[...] = jnp.zeros_like(out)

        @pl.when(core == 1)
        def _():
            out[...] = part[...]
            if rims is not None:
                for copy in near:
                    copy.wait_recv()

        if rims is not None:
            @pl.when(core == 0)
            def _():
                rpart[...] = jnp.zeros_like(rpart)

        if both:
            for d in range(1, chips):
                @pl.when(chip >= d)
                def _():
                    for e in range(2):
                        piece = pl.ds(e * half, half)
                        remote(tot.at[piece], slots.at[d - 1, piece], send_sem.at[stage, d - 1, e],
                               recv_sem.at[stage, d - 1, e], shell, patch).wait_recv()
                    out[...] += slots[d - 1]
        else:
            @pl.when(chip > 0)
            def _():
                pre[mine] = jnp.zeros((half, lanes), f32)

            for d in range(1, chips):
                @pl.when(chip >= d)
                def _():
                    for copy in sends[d - 1]:
                        copy.wait_recv()
                    pre[mine] += slots[d - 1, mine]

            @pl.when(chip > 0)
            def _():
                fwd = remote(pre.at[mine], pre.at[mine], fwd_sem.at[stage, 0], fwd_sem.at[stage, 1],
                             partner, patch)
                fwd.start()
                fwd.wait_recv()
                out[...] += pre[...]

        if rims is not None:
            for d in range(1, chips):
                @pl.when(chip >= d)
                def _():
                    for e in range(2):
                        remote(rtot.at[e], rslot.at[d - 1, e], rim_send.at[stage, d - 1, 0],
                               rim_recv.at[stage, d - 1, e], shell, patch).wait_recv()
                    rpart[...] += rslot[d - 1]

    def finish(stage, own, part, tot, slots, pre, both, rims=None):
        mine, half, first, sends = pieces(stage, own, part, tot, slots, both)
        first.wait_send()
        if rims is not None:
            near, far = rim_pieces(stage, *rims)

            @pl.when(core == 0)
            def _():
                for copy in near:
                    copy.wait_send()

        for d in range(1, chips):
            @pl.when(chip + d < chips)
            def _():
                for copy in sends[d - 1]:
                    copy.wait_send()
                if rims is not None:
                    for copy in far[d - 1]:
                        copy.wait_send()

        if not both:
            @pl.when(chip > 0)
            def _():
                remote(pre.at[mine], pre.at[mine], fwd_sem.at[stage, 0], fwd_sem.at[stage, 1],
                       partner, patch).wait_send()

    pl.semaphore_wait(barrier, 3 * shells - 1)
    b_left = remote(bedge.at[0], bhalo.at[1], edge_send.at[0], edge_recv.at[1], shell, left)
    b_right = remote(bedge.at[1], bhalo.at[0], edge_send.at[1], edge_recv.at[0], shell, right)
    b_left.start()
    b_right.start()
    rims_b = (rim_b, rtot_b, rpart_b, rslot_b)
    begin(0, sum_b, part_b, tot_b, slot_b, True, rims_b, ((0, 1), (cols - 2, cols - 1)))

    zero = jnp.zeros((cols, lanes), f32)

    def local_step(k, carry):
        se, sa, sb, sja, sjb, sba, sbb = carry
        bp[k, PAD + 8:PAD + cols - 8] = b_in[k]
        beta = jnp.concatenate([bp[k, PAD:PAD + 8], b_in[k], bp[k, PAD + cols - 8:PAD + cols]], axis=0)
        grow = jnp.exp((2.0 * step) * beta)
        es[k, inner] = grow
        dr[k, inner] = theta(beta)
        a, b = jp[0, k, inner], jp[1, k, inner]
        ja, jb = whole(barj_e, barj_in, 0, k), whole(barj_e, barj_in, 1, k)
        return (se + grow, sa + a, sb + b, sja + ja, sjb + jb, sba + beta * a, sbb + beta * b)

    se, sa, sb, sja, sjb, sba, sbb = lax.fori_loop(0, radii, local_step, (zero,) * 7, unroll=2)
    b_left.wait_recv()
    b_right.wait_recv()

    def halo_step(k, c):
        for i in range(2):
            bp[k, PAD - 2 + i:PAD - 1 + i, :] = bhalo[0, i, pl.ds(k, 1), :]
            bp[k, PAD + cols + i:PAD + cols + i + 1, :] = bhalo[1, i, pl.ds(k, 1), :]
        return c

    lax.fori_loop(0, radii, halo_step, 0, unroll=8)

    def halo_exp(k, c):
        for lo in (0, PAD + cols):
            x = bp[k, lo:lo + 8]
            es[k, lo:lo + 8] = jnp.exp((2.0 * step) * x)
            dr[k, lo:lo + 8] = theta(x)
        return c

    lax.fori_loop(0, radii, halo_exp, 0, unroll=4)
    bt[...] = jnp.zeros_like(bt)
    end(0, sum_b, part_b, tot_b, slot_b, pre_b, below_b, True, rims_b)
    bt[inner] = below_b[...]
    bt[PAD - 2:PAD] = rpart_b[0]
    bt[PAD + cols:PAD + cols + 2] = rpart_b[1]

    first = PAD - 1
    mid, hi, lo = slice(first, first + tall), slice(first + 1, first + tall + 1), slice(first - 1, first + tall - 1)
    base_r = theta(bt[mid])
    base_i = bt[hi] - bt[lo]
    base_g = step * jnp.exp((2.0 * step) * bt[mid])
    wide_zero = jnp.zeros((tall, lanes), f32)

    def u_step(k, carry):
        ua, ub = carry
        growth = base_g * es[k, mid]
        br = dr[k, mid] + base_r
        bi = 0.5 * ((bp[k, hi] - bp[k, lo]) + base_i)
        a, b = jp[0, k, mid], jp[1, k, mid]
        ua = ua + growth * (br - (a * br + b * bi))
        ub = ub + growth * (bi - (b * br - a * bi))
        up[0, k, mid] = ua
        up[1, k, mid] = ub
        return ua, ub

    ua_sum, ub_sum = lax.fori_loop(0, radii, u_step, (wide_zero, wide_zero), unroll=2)
    sum_u[:cols] = ua_sum[1:cols + 1]
    sum_u[cols:] = ub_sum[1:cols + 1]
    rims_u = (rim_u, rtot_u, rpart_u, rslot_u)
    begin(1, sum_u, part_u, tot_u, slot_u, False, rims_u, ((0, cols), (cols - 1, 2 * cols - 1)))

    full_b = bt[inner]
    grow_b = jnp.exp((2.0 * step) * full_b)

    def wh_step(k, carry):
        sw, ha, hb = carry
        beta = bp[k, inner] + full_b
        growth = grow_b * es[k, inner]
        a, b = jp[0, k, inner], jp[1, k, inner]
        ua, ub = up[0, k, inner], up[1, k, inner]
        ta, tb = theta(ua), theta(ub)
        pa = 0.5 * (up[0, k, above] - up[0, k, below])
        pb = 0.5 * (up[1, k, above] - up[1, k, below])
        ja, jb = whole(barj_e, barj_in, 0, k), whole(barj_e, barj_in, 1, k)
        sw = sw + (growth * (ta + pb) + (b * ua - a * ub))
        ha = ha + ((ta - pb) + ua * ja - ub * jb + beta * a)
        hb = hb + ((tb + pa) + ua * jb + ub * ja + beta * b)
        cw[k] = sw
        ch[0, k] = ha
        ch[1, k] = hb
        return sw, ha, hb

    sw, ha, hb = lax.fori_loop(0, radii, wh_step, (zero, zero, zero))
    end(1, sum_u, part_u, tot_u, slot_u, pre_u, below_u, False, rims_u)
    for f in range(2):
        ct[f] = jnp.zeros(ct.shape[1:], f32)
        ct[f, inner] = below_u[f * cols:(f + 1) * cols]
        ct[f, PAD - 1:PAD] = rpart_u[0, f:f + 1]
        ct[f, PAD + cols:PAD + cols + 1] = rpart_u[1, f:f + 1]
    ca, cb = ct[0, inner], ct[1, inner]
    re_bar, eth_a, eth_b = eth_planes(theta, ct, inner, above, below)
    n = float(radii)
    sum_h[:cols] = sw + (grow_b * se) * re_bar + (sb * ca - sa * cb)
    sum_h[cols:2 * cols] = ha + n * eth_a + (ca * sja - cb * sjb)
    sum_h[2 * cols:] = hb + n * eth_b + (ca * sjb + cb * sja)
    begin(2, sum_h, part_h, tot_h, slot_h, False)

    def fields_step(k, c):
        bfin[k] = step * (bp[k, inner] + full_b)
        gs[k] = grow_b * es[k, inner]
        return c

    lax.fori_loop(0, radii, fields_step, 0, unroll=2)
    end(2, sum_h, part_h, tot_h, slot_h, pre_h, below_h, False)
    b_left.wait_send()
    b_right.wait_send()
    finish(0, sum_b, part_b, tot_b, slot_b, pre_b, True, rims_b)
    finish(1, sum_u, part_u, tot_u, slot_u, pre_u, False, rims_u)
    finish(2, sum_h, part_h, tot_h, slot_h, pre_h, False)


def tail(step, jp, barj_in, barj_e, up, bfin, gs, cw, ch, ct, below_h, beta_out, u_out, w_out, h_out, uv, wv, hv, sems):
    radii, cols, lanes = cw.shape
    inner = slice(PAD, PAD + cols)
    above = slice(PAD + 1, PAD + cols + 1)
    below = slice(PAD - 1, PAD + cols - 1)
    theta = make_theta(lanes)
    copies = [pltpu.make_async_copy(bfin, beta_out, sems.at[0, 0])]
    copies[0].start()
    ca, cb = ct[0, inner], ct[1, inner]
    re_bar, eth_a, eth_b = eth_planes(theta, ct, inner, above, below)
    sq = step * step

    def final(k, carry):
        dw, da, db = carry
        a, b = jp[0, k, inner], jp[1, k, inner]
        ja, jb = whole(barj_e, barj_in, 0, k), whole(barj_e, barj_in, 1, k)
        dw = dw + (gs[k] * re_bar + (b * ca - a * cb))
        da = da + (eth_a + (ca * ja - cb * jb))
        db = db + (eth_b + (ca * jb + cb * ja))
        uv[0, k] = step * (up[0, k, inner] + ca)
        uv[1, k] = step * (up[1, k, inner] + cb)
        wv[k] = sq * (cw[k] + dw)
        hv[0, k] = sq * (ch[0, k] + da)
        hv[1, k] = sq * (ch[1, k] + db)
        return dw, da, db

    carry = tuple(below_h[i * cols:(i + 1) * cols] for i in range(3))
    chunks = sems.shape[1]
    size = radii // chunks
    for i in range(chunks):
        carry = lax.fori_loop(i * size, (i + 1) * size, final, carry, unroll=2)
        at = pl.ds(i * size, size)
        more = [pltpu.make_async_copy(uv.at[:, at], u_out.at[:, at], sems.at[1, i]),
                pltpu.make_async_copy(wv.at[at], w_out.at[at], sems.at[2, i]),
                pltpu.make_async_copy(hv.at[:, at], h_out.at[:, at], sems.at[3, i])]
        for copy in more:
            copy.start()
        copies += more
    for copy in copies:
        copy.wait()


def solution(mesh):
    shells, patches = mesh.shape["shell"], mesh.shape["patch"]
    chips = shells // 2

    def local(field_j):
        _, radii, cols, lanes = field_j.shape
        step = 1.0 / math.sqrt(radii * shells)
        f32 = jnp.float32
        vm = lambda *s: pltpu.VMEM(s, f32)
        shape = lambda *s: jax.ShapeDtypeStruct(s, f32)
        tall = cols + 2 * PAD
        dma = pltpu.SemaphoreType.DMA
        vmem = pl.BlockSpec(memory_space=pltpu.VMEM)
        hbm = pl.BlockSpec(memory_space=pltpu.HBM)
        plain, pair = (radii, cols, lanes), (2, radii, cols, lanes)
        padded, middle = (2, radii, tall, lanes), (radii, cols - 16, lanes)
        limit = 24 * 1024 * 1024
        jp, jnext, b_in, barj_in = pl.pallas_call(
            functools.partial(gather, shells, patches),
            out_shape=(shape(*padded), shape(2, cols, lanes), shape(*middle), shape(2, *middle)),
            in_specs=[hbm],
            out_specs=(vmem,) * 4,
            scratch_shapes=[vm(2, cols, lanes), vm(2, 2, radii, lanes), vm(2, 2, radii, lanes),
                            dma, dma((2,)), dma((2,)), dma((2,))],
            compiler_params=pltpu.CompilerParams(
                collective_id=0, has_side_effects=True, vmem_limit_bytes=limit),
        )(pltpu.with_memory_space_constraint(field_j, pltpu.HBM))

        many = max(chips - 1, 1)
        scratch = [vm(radii, tall, lanes)] * 3 + [vm(tall, lanes), vm(2, 2, radii, lanes), vm(2, 2, radii, lanes),
                                                  vm(cols, lanes), vm(2 * cols, lanes)]
        for n in (1, 2, 3):
            scratch += [vm(n * cols, lanes)] * 3 + [vm(many, n * cols, lanes), vm(n * cols, lanes)]
        for _ in range(2):
            scratch += [vm(2, 2, lanes)] * 3 + [vm(many, 2, 2, lanes)]
        scratch += [dma((2,)), dma((2,)), dma((3, 2)), dma((3, many, 2)), dma((3, many, 2)), dma((3, 2)),
                    dma((2, 2)), dma((2, 2)), dma((2, many, 2)), dma((2, many, 2))]
        up, bfin, gs, cw, ch, ct, below_h, barj_e = pl.pallas_call(
            functools.partial(kernel, shells, patches, step),
            out_shape=(shape(*padded), shape(*plain), shape(*plain), shape(*plain), shape(*pair),
                       shape(2, tall, lanes), shape(3 * cols, lanes), shape(2, 2, radii, 8, lanes)),
            in_specs=[vmem] * 4,
            out_specs=(vmem,) * 8,
            scratch_shapes=scratch,
            compiler_params=pltpu.CompilerParams(
                collective_id=1, has_side_effects=True, vmem_limit_bytes=limit),
        )(jp, jnext, b_in, barj_in)
        return pl.pallas_call(
            functools.partial(tail, step),
            out_shape=(shape(*plain), shape(*pair), shape(*plain), shape(*pair)),
            in_specs=[vmem] * 10,
            out_specs=(hbm,) * 4,
            scratch_shapes=[vm(*pair), vm(*plain), vm(*pair), dma((4, 4))],
            compiler_params=pltpu.CompilerParams(vmem_limit_bytes=limit),
        )(jp, barj_in, barj_e, up, bfin, gs, cw, ch, ct, below_h)

    return jax.shard_map(
        local,
        mesh=mesh,
        in_specs=(P(None, "shell", "patch", None),),
        out_specs=(
            P("shell", "patch", None),
            P(None, "shell", "patch", None),
            P("shell", "patch", None),
            P(None, "shell", "patch", None),
        ),
        check_vma=False,
    )
```

```python
import functools
import math

import jax
import jax.numpy as jnp
from jax import lax
from jax.experimental import pallas as pl
from jax.experimental.pallas import tpu as pltpu
from jax.sharding import PartitionSpec as P

PAD = 8


def remote(src, dst, send_sem, recv_sem, shell, patch):
    return pltpu.make_async_remote_copy(
        src_ref=src,
        dst_ref=dst,
        send_sem=send_sem,
        recv_sem=recv_sem,
        device_id=(shell, patch),
        device_id_type=pl.DeviceIdType.MESH,
    )


def make_theta(lanes):
    lane = lax.broadcasted_iota(jnp.int32, (8, lanes), 1)
    keep_f = jnp.where(lane == lanes - 1, 0.0, 0.5).astype(jnp.float32)
    keep_b = jnp.where(lane == 0, 0.0, 0.5).astype(jnp.float32)

    def theta(x):
        reps = x.shape[0] // 8
        mf = jnp.concatenate([keep_f] * reps, axis=0) if reps > 1 else keep_f
        mb = jnp.concatenate([keep_b] * reps, axis=0) if reps > 1 else keep_b
        return pltpu.roll(x, lanes - 1, 1) * mf - pltpu.roll(x, 1, 1) * mb

    return theta


def eth_planes(theta, pair, inner, above, below):
    ta, tb = theta(pair[0, inner]), theta(pair[1, inner])
    pa = 0.5 * (pair[0, above] - pair[0, below])
    pb = 0.5 * (pair[1, above] - pair[1, below])
    return ta + pb, ta - pb, tb + pa


def beta_terms(theta, a, b, next_a, next_b, pa, pb):
    ra, rb = next_a - a, next_b - b
    ta, tb = theta(a), theta(b)
    ea, eb = ta - pb, tb + pa
    return 0.25 * (0.5 * (ra * ra + rb * rb) - (ea * ea + eb * eb)), ta + pb, tb - pa


def kernel(shells, patches, step, j_hbm, jp, barj, up, bfin, gs, cw, ch, ct, below_h,
           bp, es, dr, bt, bedge, bhalo, below_b, below_u, jnext, jedge, jside, jhalo, rows_w,
           sum_b, part_b, tot_b, slot_b, pre_b,
           sum_u, part_u, tot_u, slot_u, pre_u,
           sum_h, part_h, tot_h, slot_h, pre_h,
           rim_b, rtot_b, rpart_b, rslot_b, rim_u, rtot_u, rpart_u, rslot_u,
           load_sem, rad_sem, jh_send, jh_recv, up_ready, side_ready,
           edge_send, edge_recv, part_sem, send_sem, recv_sem, fwd_sem,
           rpart_send, rpart_recv, rim_send, rim_recv):
    radii, cols, lanes = cw.shape
    tall = cols + 8
    f32 = jnp.float32
    chips = shells // 2
    shell, patch = lax.axis_index("shell"), lax.axis_index("patch")
    chip, core = shell // 2, shell % 2
    partner = shell + 1 - 2 * core
    right = lax.rem(patch + 1, patches)
    left = lax.rem(patch + patches - 1, patches)
    inner = slice(PAD, PAD + cols)
    above = slice(PAD + 1, PAD + cols + 1)
    below = slice(PAD - 1, PAD + cols - 1)
    before, after = slice(PAD - 1, PAD), slice(PAD + cols, PAD + cols + 1)
    theta = make_theta(lanes)
    mesh_id = pl.DeviceIdType.MESH

    load = pltpu.make_async_copy(j_hbm, jp.at[:, :, pl.ds(PAD, cols), :], load_sem)
    load.start()

    barrier = pltpu.get_barrier_semaphore()
    def greet(there, p):
        pl.semaphore_signal(barrier, inc=1, device_id=(there, p), device_id_type=mesh_id)

    greet(partner, patch)
    greet(shell, left)
    greet(shell, right)

    @pl.when(chip > 0)
    def _():
        greet(shell - 2, patch)

        @pl.when(core == 0)
        def _():
            greet(shell - 1, patch)

    @pl.when(chip < chips - 1)
    def _():
        greet(shell + 2, patch)

        @pl.when(core == 1)
        def _():
            greet(shell + 1, patch)

    load.wait()

    def pack(k, c):
        for f in range(2):
            jedge[0, f, pl.ds(k, 1), :] = jp[f, k, PAD:PAD + 1, :]
            jedge[1, f, pl.ds(k, 1), :] = jp[f, k, PAD + cols - 1:PAD + cols, :]
        return c

    lax.fori_loop(0, radii, pack, 0, unroll=8)
    inside, outside = (chip > 0).astype(jnp.int32), (chip < chips - 1).astype(jnp.int32)
    pl.semaphore_wait(barrier, 3 + inside * (2 - core) + outside * (1 + core))
    to_left = remote(jedge.at[0, :, pl.ds(0, radii)], jhalo.at[1], jh_send.at[0], jh_recv.at[1], shell, left)
    to_right = remote(jedge.at[1, :, pl.ds(0, radii)], jhalo.at[0], jh_send.at[1], jh_recv.at[0], shell, right)
    to_left.start()
    to_right.start()

    def chain(step_at):
        @pl.when(step_at)
        def _():
            @pl.when(chip < chips - 1)
            def _():
                pl.semaphore_wait(up_ready, 1)

            @pl.when(chip > 0)
            def _():
                pl.semaphore_signal(up_ready, inc=1, device_id=(shell - 2, patch), device_id_type=mesh_id)

            pl.semaphore_signal(side_ready, inc=1, device_id=(partner, patch), device_id_type=mesh_id)

    chain(chip == chips - 1)

    def down(there):
        return remote(j_hbm.at[:, 0], jnext, rad_sem.at[0], rad_sem.at[1], there, patch)

    @pl.when(shell > 0)
    def _():
        down(shell - 1).start()

    def pack_side(k, c):
        for f in range(2):
            jside[0, f, pl.ds(k, 1), :] = jp[f, k, PAD + 1:PAD + 2, :]
            jside[1, f, pl.ds(k, 1), :] = jp[f, k, PAD + cols - 2:PAD + cols - 1, :]
        return c

    lax.fori_loop(0, radii, pack_side, 0, unroll=8)

    def beta_step(k, next_a, next_b, total):
        pa = 0.5 * (jp[0, k, above] - jp[0, k, below])
        pb = 0.5 * (jp[1, k, above] - jp[1, k, below])
        source, ja, jb = beta_terms(theta, jp[0, k, inner], jp[1, k, inner], next_a, next_b, pa, pb)
        barj[0, k], barj[1, k] = ja, jb
        total = total + source
        bp[k, inner] = total
        bedge[0, 1, pl.ds(k, 1), :] = total[1:2]
        bedge[1, 0, pl.ds(k, 1), :] = total[cols - 2:cols - 1]
        return total

    zero = jnp.zeros((cols, lanes), f32)
    total = zero
    slices = 4
    for i in range(slices):
        stop = (i + 1) * radii // slices if i < slices - 1 else radii - 1
        total = lax.fori_loop(
            i * radii // slices, stop,
            lambda k, t: beta_step(k, jp[0, k + 1, inner], jp[1, k + 1, inner], t), total, unroll=2)
        if i < slices - 1:
            chain(chip == chips - 2 - i)
    for c in range(chips - 1 - slices, -1, -1):
        chain(chip == c)

    @pl.when(shell == shells - 1)
    def _():
        for f in range(2):
            jnext[f] = jp[f, radii - 1, inner]

    @pl.when(shell < shells - 1)
    def _():
        down(shell).wait_recv()

    sum_b[...] = beta_step(radii - 1, jnext[0], jnext[1], total)
    for f in range(2):
        jedge[0, f, radii:radii + 1] = jnext[f, 0:1]
        jedge[1, f, radii:radii + 1] = jnext[f, cols - 1:cols]
    to_left.wait_recv()
    to_right.wait_recv()
    edge_sources = []
    for side, (over, under) in enumerate(((jside.at[0], jhalo.at[0]), (jhalo.at[1], jside.at[1]))):
        pa, pb = (0.5 * (over[f] - under[f]) for f in range(2))
        source, ja, jb = beta_terms(
            theta, jedge[side, 0, 0:radii], jedge[side, 1, 0:radii],
            jedge[side, 0, 1:radii + 1], jedge[side, 1, 1:radii + 1], pa, pb)
        rows_w[side, 0], rows_w[side, 1] = ja, jb
        edge_sources.append(source)
        at = side * (cols - 1)
        sum_b[at:at + 1] = jnp.sum(source, axis=0, keepdims=True)

    def pieces(stage, own, part, tot, slots, both):
        half = own.shape[0] // 2
        mine = pl.ds(pl.multiple_of(core * half, 8), half)
        first = remote(own, part, part_sem.at[stage, 0], part_sem.at[stage, 1], partner, patch)
        sends = []
        for d in range(1, chips):
            if both:
                sends.append([
                    remote(tot.at[mine], slots.at[d - 1, mine], send_sem.at[stage, d - 1, e],
                           recv_sem.at[stage, d - 1, core], (chip + d) * 2 + e, patch)
                    for e in range(2)])
            else:
                sends.append([
                    remote(tot.at[mine], slots.at[d - 1, mine], send_sem.at[stage, d - 1, 0],
                           recv_sem.at[stage, d - 1, 0], (chip + d) * 2 + core, patch)])
        return mine, half, first, sends

    def rim_pieces(stage, rim, rtot, rpart, rslot):
        over = left * (1 - core) + right * core
        near = [
            remote(rim.at[0], rpart.at[1], rpart_send.at[stage, 0], rpart_recv.at[stage, 1], partner, left),
            remote(rim.at[1], rpart.at[0], rpart_send.at[stage, 1], rpart_recv.at[stage, 0], partner, right)]
        far = [[
            remote(rtot.at[core], rslot.at[d - 1, 1 - core], rim_send.at[stage, d - 1, e],
                   rim_recv.at[stage, d - 1, 1 - core], (chip + d) * 2 + e, over)
            for e in range(2)] for d in range(1, chips)]
        return near, far

    def begin(stage, own, part, tot, slots, both, during, rims=None, lines=None):
        mine, half, first, sends = pieces(stage, own, part, tot, slots, both)
        first.start()
        if rims is not None:
            rim, rtot, rpart, rslot = rims
            for side in range(2):
                for i, r in enumerate(lines[side]):
                    rim[side, i:i + 1] = own[r:r + 1]
            near, far = rim_pieces(stage, rim, rtot, rpart, rslot)

            @pl.when(core == 0)
            def _():
                for copy in near:
                    copy.start()

        during()
        first.wait_recv()
        tot[mine] = own[mine] + part[mine]
        if rims is not None:
            for side in range(2):
                for i, r in enumerate(lines[side]):
                    rtot[side, i:i + 1] = own[r:r + 1] + part[r:r + 1]
        for d in range(1, chips):
            @pl.when(chip + d < chips)
            def _():
                for copy in sends[d - 1]:
                    copy.start()
                if rims is not None:
                    for copy in far[d - 1]:
                        copy.start()

    def end(stage, own, part, tot, slots, pre, out, both, rims=None):
        mine, half, first, sends = pieces(stage, own, part, tot, slots, both)
        if rims is not None:
            rim, rtot, rpart, rslot = rims
            near, far = rim_pieces(stage, rim, rtot, rpart, rslot)

        @pl.when(core == 0)
        def _():
            out[...] = jnp.zeros_like(out)

        @pl.when(core == 1)
        def _():
            out[...] = part[...]
            if rims is not None:
                for copy in near:
                    copy.wait_recv()

        if rims is not None:
            @pl.when(core == 0)
            def _():
                rpart[...] = jnp.zeros_like(rpart)

        if both:
            for d in range(1, chips):
                @pl.when(chip >= d)
                def _():
                    for e in range(2):
                        piece = pl.ds(e * half, half)
                        remote(tot.at[piece], slots.at[d - 1, piece], send_sem.at[stage, d - 1, e],
                               recv_sem.at[stage, d - 1, e], shell, patch).wait_recv()
                    out[...] += slots[d - 1]
        else:
            @pl.when(chip > 0)
            def _():
                pre[mine] = jnp.zeros((half, lanes), f32)

            for d in range(1, chips):
                @pl.when(chip >= d)
                def _():
                    for copy in sends[d - 1]:
                        copy.wait_recv()
                    pre[mine] += slots[d - 1, mine]

            @pl.when(chip > 0)
            def _():
                fwd = remote(pre.at[mine], pre.at[mine], fwd_sem.at[stage, 0], fwd_sem.at[stage, 1],
                             partner, patch)
                fwd.start()
                fwd.wait_recv()
                out[...] += pre[...]

        if rims is not None:
            for d in range(1, chips):
                @pl.when(chip >= d)
                def _():
                    for e in range(2):
                        remote(rtot.at[e], rslot.at[d - 1, e], rim_send.at[stage, d - 1, 0],
                               rim_recv.at[stage, d - 1, e], shell, patch).wait_recv()
                    rpart[...] += rslot[d - 1]

    def finish(stage, own, part, tot, slots, pre, both, rims=None):
        mine, half, first, sends = pieces(stage, own, part, tot, slots, both)
        first.wait_send()
        if rims is not None:
            near, far = rim_pieces(stage, *rims)

            @pl.when(core == 0)
            def _():
                for copy in near:
                    copy.wait_send()

        for d in range(1, chips):
            @pl.when(chip + d < chips)
            def _():
                for copy in sends[d - 1]:
                    copy.wait_send()
                if rims is not None:
                    for copy in far[d - 1]:
                        copy.wait_send()

        if not both:
            @pl.when(chip > 0)
            def _():
                remote(pre.at[mine], pre.at[mine], fwd_sem.at[stage, 0], fwd_sem.at[stage, 1],
                       partner, patch).wait_send()

    pl.semaphore_wait(side_ready, 1)
    b_left = remote(bedge.at[0], bhalo.at[1], edge_send.at[0], edge_recv.at[1], shell, left)
    b_right = remote(bedge.at[1], bhalo.at[0], edge_send.at[1], edge_recv.at[0], shell, right)

    def finish_edges():
        row = lax.broadcasted_iota(jnp.int32, (radii, lanes), 0)
        for side in range(2):
            x, shift = edge_sources[side], 1
            while shift < radii:
                x = x + jnp.where(row >= shift, pltpu.roll(x, shift, 0), 0.0)
                shift *= 2
            bedge[side, side] = x
        b_left.start()
        b_right.start()

        def place(k, c):
            for side in range(2):
                at = side * (cols - 1)
                bp[k, PAD + at:PAD + at + 1, :] = bedge[side, side, pl.ds(k, 1), :]
                for f in range(2):
                    barj[f, k, at:at + 1, :] = rows_w[side, f, pl.ds(k, 1), :]
            for f in range(2):
                jp[f, k, before, :] = jhalo[0, f, pl.ds(k, 1), :]
                jp[f, k, after, :] = jhalo[1, f, pl.ds(k, 1), :]
            return c

        lax.fori_loop(0, radii, place, 0, unroll=4)

    rims_b = (rim_b, rtot_b, rpart_b, rslot_b)
    begin(0, sum_b, part_b, tot_b, slot_b, True, finish_edges, rims_b, ((0, 1), (cols - 2, cols - 1)))

    def local_step(k, carry):
        se, sa, sb, sja, sjb = carry
        beta = bp[k, inner]
        grow = jnp.exp((2.0 * step) * beta)
        es[k, inner] = grow
        dr[k, inner] = theta(beta)
        a, b = jp[0, k, inner], jp[1, k, inner]
        return (se + grow, sa + a, sb + b, sja + barj[0, k], sjb + barj[1, k])

    se, sa, sb, sja, sjb = lax.fori_loop(0, radii, local_step, (zero,) * 5, unroll=2)
    b_left.wait_recv()
    b_right.wait_recv()

    def halo_step(k, c):
        for i in range(2):
            bp[k, PAD - 2 + i:PAD - 1 + i, :] = bhalo[0, i, pl.ds(k, 1), :]
            bp[k, PAD + cols + i:PAD + cols + i + 1, :] = bhalo[1, i, pl.ds(k, 1), :]
        return c

    lax.fori_loop(0, radii, halo_step, 0, unroll=8)

    def halo_exp(k, c):
        for lo in (0, PAD + cols):
            x = bp[k, lo:lo + 8]
            es[k, lo:lo + 8] = jnp.exp((2.0 * step) * x)
            dr[k, lo:lo + 8] = theta(x)
        return c

    lax.fori_loop(0, radii, halo_exp, 0, unroll=4)
    bt[...] = jnp.zeros_like(bt)
    end(0, sum_b, part_b, tot_b, slot_b, pre_b, below_b, True, rims_b)
    bt[inner] = below_b[...]
    bt[PAD - 2:PAD] = rpart_b[0]
    bt[PAD + cols:PAD + cols + 2] = rpart_b[1]

    first = PAD - 1
    mid, hi, lo = slice(first, first + tall), slice(first + 1, first + tall + 1), slice(first - 1, first + tall - 1)
    base_r = theta(bt[mid])
    base_i = bt[hi] - bt[lo]
    base_g = step * jnp.exp((2.0 * step) * bt[mid])
    wide_zero = jnp.zeros((tall, lanes), f32)

    def u_step(k, carry):
        ua, ub = carry
        growth = base_g * es[k, mid]
        br = dr[k, mid] + base_r
        bi = 0.5 * ((bp[k, hi] - bp[k, lo]) + base_i)
        a, b = jp[0, k, mid], jp[1, k, mid]
        ua = ua + growth * (br - (a * br + b * bi))
        ub = ub + growth * (bi - (b * br - a * bi))
        up[0, k, mid] = ua
        up[1, k, mid] = ub
        return ua, ub

    ua_sum, ub_sum = lax.fori_loop(0, radii, u_step, (wide_zero, wide_zero), unroll=2)
    sum_u[:cols] = ua_sum[1:cols + 1]
    sum_u[cols:] = ub_sum[1:cols + 1]
    full_b = bt[inner]
    grow_b = jnp.exp((2.0 * step) * full_b)

    def wh_step(k, carry):
        sw, ha, hb = carry
        beta = bp[k, inner] + full_b
        growth = grow_b * es[k, inner]
        a, b = jp[0, k, inner], jp[1, k, inner]
        ua, ub = up[0, k, inner], up[1, k, inner]
        ta, tb = theta(ua), theta(ub)
        pa = 0.5 * (up[0, k, above] - up[0, k, below])
        pb = 0.5 * (up[1, k, above] - up[1, k, below])
        ja, jb = barj[0, k], barj[1, k]
        sw = sw + (growth * (ta + pb) + (b * ua - a * ub))
        ha = ha + ((ta - pb) + ua * ja - ub * jb + beta * a)
        hb = hb + ((tb + pa) + ua * jb + ub * ja + beta * b)
        cw[k] = sw
        ch[0, k] = ha
        ch[1, k] = hb
        return sw, ha, hb

    done = []
    ahead = radii // 4
    rims_u = (rim_u, rtot_u, rpart_u, rslot_u)
    begin(1, sum_u, part_u, tot_u, slot_u, False,
          lambda: done.extend(lax.fori_loop(0, ahead, wh_step, (zero, zero, zero))),
          rims_u, ((0, cols), (cols - 1, 2 * cols - 1)))
    sw, ha, hb = lax.fori_loop(ahead, radii, wh_step, tuple(done))
    end(1, sum_u, part_u, tot_u, slot_u, pre_u, below_u, False, rims_u)
    for f in range(2):
        ct[f] = jnp.zeros(ct.shape[1:], f32)
        ct[f, inner] = below_u[f * cols:(f + 1) * cols]
        ct[f, PAD - 1:PAD] = rpart_u[0, f:f + 1]
        ct[f, PAD + cols:PAD + cols + 1] = rpart_u[1, f:f + 1]
    ca, cb = ct[0, inner], ct[1, inner]
    re_bar, eth_a, eth_b = eth_planes(theta, ct, inner, above, below)
    n = float(radii)
    sum_h[:cols] = sw + (grow_b * se) * re_bar + (sb * ca - sa * cb)
    sum_h[cols:2 * cols] = ha + n * eth_a + (ca * sja - cb * sjb)
    sum_h[2 * cols:] = hb + n * eth_b + (ca * sjb + cb * sja)

    def fields_step(k, c):
        bfin[k] = step * (bp[k, inner] + full_b)
        gs[k] = grow_b * es[k, inner]
        return c

    begin(2, sum_h, part_h, tot_h, slot_h, False, lambda: lax.fori_loop(0, radii, fields_step, 0, unroll=2))
    end(2, sum_h, part_h, tot_h, slot_h, pre_h, below_h, False)
    to_left.wait_send()
    to_right.wait_send()

    @pl.when(shell > 0)
    def _():
        down(shell - 1).wait_send()

    b_left.wait_send()
    b_right.wait_send()
    finish(0, sum_b, part_b, tot_b, slot_b, pre_b, True, rims_b)
    finish(1, sum_u, part_u, tot_u, slot_u, pre_u, False, rims_u)
    finish(2, sum_h, part_h, tot_h, slot_h, pre_h, False)


def tail(step, jp, barj, up, bfin, gs, cw, ch, ct, below_h, beta_out, u_out, w_out, h_out, uv, wv, hv, sems):
    radii, cols, lanes = cw.shape
    inner = slice(PAD, PAD + cols)
    above = slice(PAD + 1, PAD + cols + 1)
    below = slice(PAD - 1, PAD + cols - 1)
    theta = make_theta(lanes)
    copies = [pltpu.make_async_copy(bfin, beta_out, sems.at[0, 0])]
    copies[0].start()
    ca, cb = ct[0, inner], ct[1, inner]
    re_bar, eth_a, eth_b = eth_planes(theta, ct, inner, above, below)
    sq = step * step

    def final(k, carry):
        dw, da, db = carry
        a, b = jp[0, k, inner], jp[1, k, inner]
        ja, jb = barj[0, k], barj[1, k]
        dw = dw + (gs[k] * re_bar + (b * ca - a * cb))
        da = da + (eth_a + (ca * ja - cb * jb))
        db = db + (eth_b + (ca * jb + cb * ja))
        uv[0, k] = step * (up[0, k, inner] + ca)
        uv[1, k] = step * (up[1, k, inner] + cb)
        wv[k] = sq * (cw[k] + dw)
        hv[0, k] = sq * (ch[0, k] + da)
        hv[1, k] = sq * (ch[1, k] + db)
        return dw, da, db

    carry = tuple(below_h[i * cols:(i + 1) * cols] for i in range(3))
    chunks = sems.shape[1]
    size = radii // chunks
    for i in range(chunks):
        carry = lax.fori_loop(i * size, (i + 1) * size, final, carry, unroll=2)
        at = pl.ds(i * size, size)
        more = [pltpu.make_async_copy(uv.at[:, at], u_out.at[:, at], sems.at[1, i]),
                pltpu.make_async_copy(wv.at[at], w_out.at[at], sems.at[2, i]),
                pltpu.make_async_copy(hv.at[:, at], h_out.at[:, at], sems.at[3, i])]
        for copy in more:
            copy.start()
        copies += more
    for copy in copies:
        copy.wait()


def solution(mesh):
    shells, patches = mesh.shape["shell"], mesh.shape["patch"]
    chips = shells // 2

    def local(field_j):
        _, radii, cols, lanes = field_j.shape
        step = 1.0 / math.sqrt(radii * shells)
        f32 = jnp.float32
        vm = lambda *s: pltpu.VMEM(s, f32)
        shape = lambda *s: jax.ShapeDtypeStruct(s, f32)
        tall = cols + 2 * PAD
        dma = pltpu.SemaphoreType.DMA
        vmem = pl.BlockSpec(memory_space=pltpu.VMEM)
        hbm = pl.BlockSpec(memory_space=pltpu.HBM)
        plain, pair = (radii, cols, lanes), (2, radii, cols, lanes)
        padded = (2, radii, tall, lanes)
        limit = 24 * 1024 * 1024
        many = max(chips - 1, 1)
        regular = pltpu.SemaphoreType.REGULAR
        planes = vm(2, 2, radii, lanes)
        scratch = [vm(radii, tall, lanes)] * 3 + [vm(tall, lanes), planes, planes, vm(cols, lanes), vm(2 * cols, lanes),
                                                  vm(2, cols, lanes), vm(2, 2, radii + 8, lanes), planes, planes, planes]
        for n in (1, 2, 3):
            scratch += [vm(n * cols, lanes)] * 3 + [vm(many, n * cols, lanes), vm(n * cols, lanes)]
        for _ in range(2):
            scratch += [vm(2, 2, lanes)] * 3 + [vm(many, 2, 2, lanes)]
        scratch += [dma, dma((2,)), dma((2,)), dma((2,)), regular, regular,
                    dma((2,)), dma((2,)), dma((3, 2)), dma((3, many, 2)), dma((3, many, 2)), dma((3, 2)),
                    dma((2, 2)), dma((2, 2)), dma((2, many, 2)), dma((2, many, 2))]
        found = pl.pallas_call(
            functools.partial(kernel, shells, patches, step),
            out_shape=(shape(*padded), shape(*pair), shape(*padded), shape(*plain), shape(*plain), shape(*plain),
                       shape(*pair), shape(2, tall, lanes), shape(3 * cols, lanes)),
            in_specs=[hbm],
            out_specs=(vmem,) * 9,
            scratch_shapes=scratch,
            compiler_params=pltpu.CompilerParams(
                collective_id=0, has_side_effects=True, vmem_limit_bytes=limit),
        )(pltpu.with_memory_space_constraint(field_j, pltpu.HBM))
        return pl.pallas_call(
            functools.partial(tail, step),
            out_shape=(shape(*plain), shape(*pair), shape(*plain), shape(*pair)),
            in_specs=[vmem] * 9,
            out_specs=(hbm,) * 4,
            scratch_shapes=[vm(*pair), vm(*plain), vm(*pair), dma((4, 4))],
            compiler_params=pltpu.CompilerParams(vmem_limit_bytes=limit),
        )(*found)

    return jax.shard_map(
        local,
        mesh=mesh,
        in_specs=(P(None, "shell", "patch", None),),
        out_specs=(
            P("shell", "patch", None),
            P(None, "shell", "patch", None),
            P("shell", "patch", None),
            P(None, "shell", "patch", None),
        ),
        check_vma=False,
    )
```

```python
import functools
import math

import jax
import jax.numpy as jnp
from jax import lax
from jax.experimental import pallas as pl
from jax.experimental.pallas import tpu as pltpu
from jax.sharding import PartitionSpec as P

PAD = 8


def remote(src, dst, send_sem, recv_sem, shell, patch):
    return pltpu.make_async_remote_copy(
        src_ref=src,
        dst_ref=dst,
        send_sem=send_sem,
        recv_sem=recv_sem,
        device_id=(shell, patch),
        device_id_type=pl.DeviceIdType.MESH,
    )


def make_theta(lanes):
    lane = lax.broadcasted_iota(jnp.int32, (8, lanes), 1)
    keep_f = jnp.where(lane == lanes - 1, 0.0, 0.5).astype(jnp.float32)
    keep_b = jnp.where(lane == 0, 0.0, 0.5).astype(jnp.float32)

    def theta(x):
        reps = x.shape[0] // 8
        mf = jnp.concatenate([keep_f] * reps, axis=0) if reps > 1 else keep_f
        mb = jnp.concatenate([keep_b] * reps, axis=0) if reps > 1 else keep_b
        return pltpu.roll(x, lanes - 1, 1) * mf - pltpu.roll(x, 1, 1) * mb

    return theta


def eth_planes(theta, pair, inner, above, below):
    ta, tb = theta(pair[0, inner]), theta(pair[1, inner])
    pa = 0.5 * (pair[0, above] - pair[0, below])
    pb = 0.5 * (pair[1, above] - pair[1, below])
    return ta + pb, ta - pb, tb + pa


def beta_terms(theta, a, b, next_a, next_b, pa, pb):
    ra, rb = next_a - a, next_b - b
    ta, tb = theta(a), theta(b)
    ea, eb = ta - pb, tb + pa
    return 0.25 * (0.5 * (ra * ra + rb * rb) - (ea * ea + eb * eb)), ta + pb, tb - pa


def kernel(shells, patches, step, j_hbm, bfin, ufin, cw, ch, below_h,
           jp, barj, up, ct, bp, es, dr, bt, bedge, bhalo, below_b, below_u, jnext, jedge, jside, jhalo, rows_w,
           sum_b, part_b, tot_b, slot_b,
           sum_u, part_u, tot_u, slot_u,
           sum_h, part_h, tot_h, slot_h,
           rim_b, rtot_b, rpart_b, rslot_b, rim_u, rtot_u, rpart_u, rslot_u,
           load_sem, rad_sem, jh_send, jh_recv, up_ready, side_ready,
           edge_recv, part_send, part_recv, send_sem, recv_sem,
           rpart_send, rpart_recv, rim_send, rim_recv):
    radii, cols, lanes = cw.shape
    tall = cols + 8
    f32 = jnp.float32
    chips = shells // 2
    shell, patch = lax.axis_index("shell"), lax.axis_index("patch")
    chip, core = shell // 2, shell % 2
    partner = shell + 1 - 2 * core
    right = lax.rem(patch + 1, patches)
    left = lax.rem(patch + patches - 1, patches)
    inner = slice(PAD, PAD + cols)
    above = slice(PAD + 1, PAD + cols + 1)
    below = slice(PAD - 1, PAD + cols - 1)
    before, after = slice(PAD - 1, PAD), slice(PAD + cols, PAD + cols + 1)
    theta = make_theta(lanes)
    mesh_id = pl.DeviceIdType.MESH

    load = pltpu.make_async_copy(j_hbm, jp.at[:, :, pl.ds(PAD, cols), :], load_sem)
    load.start()

    barrier = pltpu.get_barrier_semaphore()
    def greet(there, p):
        pl.semaphore_signal(barrier, inc=1, device_id=(there, p), device_id_type=mesh_id)

    greet(partner, patch)
    greet(shell, left)
    greet(shell, right)

    @pl.when(chip > 0)
    def _():
        greet(shell - 2, patch)

        @pl.when(core == 0)
        def _():
            greet(shell - 1, patch)

    @pl.when(chip < chips - 1)
    def _():
        greet(shell + 2, patch)

        @pl.when(core == 1)
        def _():
            greet(shell + 1, patch)

    load.wait()

    def pack(k, c):
        for f in range(2):
            jedge[0, f, pl.ds(k, 1), :] = jp[f, k, PAD:PAD + 1, :]
            jedge[1, f, pl.ds(k, 1), :] = jp[f, k, PAD + cols - 1:PAD + cols, :]
        return c

    lax.fori_loop(0, radii, pack, 0, unroll=8)
    inside, outside = (chip > 0).astype(jnp.int32), (chip < chips - 1).astype(jnp.int32)
    pl.semaphore_wait(barrier, 3 + inside * (2 - core) + outside * (1 + core))
    to_left = remote(jedge.at[0, :, pl.ds(0, radii)], jhalo.at[1], jh_send.at[0], jh_recv.at[1], shell, left)
    to_right = remote(jedge.at[1, :, pl.ds(0, radii)], jhalo.at[0], jh_send.at[1], jh_recv.at[0], shell, right)
    to_left.start()
    to_right.start()

    def chain(step_at):
        @pl.when(step_at)
        def _():
            @pl.when(chip < chips - 1)
            def _():
                pl.semaphore_wait(up_ready, 1)

            @pl.when(chip > 0)
            def _():
                pl.semaphore_signal(up_ready, inc=1, device_id=(shell - 2, patch), device_id_type=mesh_id)

            pl.semaphore_signal(side_ready, inc=1, device_id=(partner, patch), device_id_type=mesh_id)

    chain(chip == chips - 1)

    def down(there):
        return remote(j_hbm.at[:, 0], jnext, rad_sem.at[0], rad_sem.at[1], there, patch)

    @pl.when(shell > 0)
    def _():
        down(shell - 1).start()

    def pack_side(k, c):
        for f in range(2):
            jside[0, f, pl.ds(k, 1), :] = jp[f, k, PAD + 1:PAD + 2, :]
            jside[1, f, pl.ds(k, 1), :] = jp[f, k, PAD + cols - 2:PAD + cols - 1, :]
        return c

    lax.fori_loop(0, radii, pack_side, 0, unroll=8)

    def beta_step(k, next_a, next_b, total):
        pa = 0.5 * (jp[0, k, above] - jp[0, k, below])
        pb = 0.5 * (jp[1, k, above] - jp[1, k, below])
        source, ja, jb = beta_terms(theta, jp[0, k, inner], jp[1, k, inner], next_a, next_b, pa, pb)
        barj[0, k], barj[1, k] = ja, jb
        total = total + source
        bp[k, inner] = total
        bedge[0, 1, pl.ds(k, 1), :] = total[1:2]
        bedge[1, 0, pl.ds(k, 1), :] = total[cols - 2:cols - 1]
        return total

    zero = jnp.zeros((cols, lanes), f32)
    total = zero
    slices = 4
    for i in range(slices):
        stop = (i + 1) * radii // slices if i < slices - 1 else radii - 1
        total = lax.fori_loop(
            i * radii // slices, stop,
            lambda k, t: beta_step(k, jp[0, k + 1, inner], jp[1, k + 1, inner], t), total, unroll=2)
        if i == slices // 2 - 1 and chips > 1:
            chain(chip == chips - 2)

    @pl.when(shell == shells - 1)
    def _():
        for f in range(2):
            jnext[f] = jp[f, radii - 1, inner]

    @pl.when(shell < shells - 1)
    def _():
        down(shell).wait_recv()

    sum_b[...] = beta_step(radii - 1, jnext[0], jnext[1], total)
    for f in range(2):
        jedge[0, f, radii:radii + 1] = jnext[f, 0:1]
        jedge[1, f, radii:radii + 1] = jnext[f, cols - 1:cols]
    for c in range(chips - 3, 0, -1):
        chain(chip == c)
    to_left.wait_recv()
    to_right.wait_recv()
    to_left.wait_send()
    to_right.wait_send()
    edge_sources = []
    for side, (over, under) in enumerate(((jside.at[0], jhalo.at[0]), (jhalo.at[1], jside.at[1]))):
        pa, pb = (0.5 * (over[f] - under[f]) for f in range(2))
        source, ja, jb = beta_terms(
            theta, jedge[side, 0, 0:radii], jedge[side, 1, 0:radii],
            jedge[side, 0, 1:radii + 1], jedge[side, 1, 1:radii + 1], pa, pb)
        rows_w[side, 0], rows_w[side, 1] = ja, jb
        edge_sources.append(source)
        at = side * (cols - 1)
        sum_b[at:at + 1] = jnp.sum(source, axis=0, keepdims=True)

    def pieces(stage, own, part, tot, slots):
        half = own.shape[0] // 2
        mine = pl.ds(pl.multiple_of(core * half, 8), half)
        first = remote(own, part, part_send, part_recv.at[stage], partner, patch)
        sends = [[
            remote(tot.at[mine], slots.at[d - 1, mine], send_sem.at[d - 1, e],
                   recv_sem.at[stage, d - 1, core], (chip + d) * 2 + e, patch)
            for e in range(2)] for d in range(1, chips)]
        return mine, half, first, sends

    def rim_pieces(stage, rim, rtot, rpart, rslot):
        over = left * (1 - core) + right * core
        near = [
            remote(rim.at[0], rpart.at[1], rpart_send.at[0], rpart_recv.at[stage, 1], partner, left),
            remote(rim.at[1], rpart.at[0], rpart_send.at[1], rpart_recv.at[stage, 0], partner, right)]
        far = [[
            remote(rtot.at[core], rslot.at[d - 1, 1 - core], rim_send.at[d - 1, e],
                   rim_recv.at[stage, d - 1, 1 - core], (chip + d) * 2 + e, over)
            for e in range(2)] for d in range(1, chips)]
        return near, far

    def begin(stage, own, part, tot, slots, during, rims=None, lines=None):
        mine, half, first, sends = pieces(stage, own, part, tot, slots)
        first.start()
        if rims is not None:
            rim, rtot, rpart, rslot = rims
            for side in range(2):
                for i, r in enumerate(lines[side]):
                    rim[side, i:i + 1] = own[r:r + 1]
            near, far = rim_pieces(stage, rim, rtot, rpart, rslot)

            @pl.when(core == 0)
            def _():
                for copy in near:
                    copy.start()

        during()
        first.wait_recv()
        tot[mine] = own[mine] + part[mine]
        if rims is not None:
            for side in range(2):
                for i, r in enumerate(lines[side]):
                    rtot[side, i:i + 1] = own[r:r + 1] + part[r:r + 1]
        for d in range(chips - 1, 0, -1):
            @pl.when(chip + d < chips)
            def _():
                for copy in sends[d - 1]:
                    copy.start()
                if rims is not None:
                    for copy in far[d - 1]:
                        copy.start()

    def end(stage, own, part, tot, slots, out, rims=None):
        mine, half, first, sends = pieces(stage, own, part, tot, slots)
        if rims is not None:
            rim, rtot, rpart, rslot = rims
            near, far = rim_pieces(stage, rim, rtot, rpart, rslot)

        @pl.when(core == 0)
        def _():
            out[...] = jnp.zeros_like(out)

        @pl.when(core == 1)
        def _():
            out[...] = part[...]
            if rims is not None:
                for copy in near:
                    copy.wait_recv()

        if rims is not None:
            @pl.when(core == 0)
            def _():
                rpart[...] = jnp.zeros_like(rpart)

        for d in range(1, chips):
            @pl.when(chip >= d)
            def _():
                for e in range(2):
                    piece = pl.ds(e * half, half)
                    remote(tot.at[piece], slots.at[d - 1, piece], send_sem.at[d - 1, e],
                           recv_sem.at[stage, d - 1, e], shell, patch).wait_recv()
                out[...] += slots[d - 1]

        if rims is not None:
            for d in range(1, chips):
                @pl.when(chip >= d)
                def _():
                    for e in range(2):
                        remote(rtot.at[e], rslot.at[d - 1, e], rim_send.at[d - 1, 0],
                               rim_recv.at[stage, d - 1, e], shell, patch).wait_recv()
                    rpart[...] += rslot[d - 1]

    def finish(stage, own, part, tot, slots, rims=None):
        mine, half, first, sends = pieces(stage, own, part, tot, slots)
        first.wait_send()
        if rims is not None:
            near, far = rim_pieces(stage, *rims)

            @pl.when(core == 0)
            def _():
                for copy in near:
                    copy.wait_send()

        for d in range(1, chips):
            @pl.when(chip + d < chips)
            def _():
                for copy in sends[d - 1]:
                    copy.wait_send()
                if rims is not None:
                    for copy in far[d - 1]:
                        copy.wait_send()

    if chips > 2:
        chain(chip == 0)
    pl.semaphore_wait(side_ready, 1)
    b_left = remote(bedge.at[0], bhalo.at[1], jh_send.at[0], edge_recv.at[1], shell, left)
    b_right = remote(bedge.at[1], bhalo.at[0], jh_send.at[1], edge_recv.at[0], shell, right)

    def finish_edges():
        row = lax.broadcasted_iota(jnp.int32, (radii, lanes), 0)
        for side in range(2):
            x, shift = edge_sources[side], 1
            while shift < radii:
                x = x + jnp.where(row >= shift, pltpu.roll(x, shift, 0), 0.0)
                shift *= 2
            bedge[side, side] = x
        b_left.start()
        b_right.start()

        def place(k, c):
            for side in range(2):
                at = side * (cols - 1)
                bp[k, PAD + at:PAD + at + 1, :] = bedge[side, side, pl.ds(k, 1), :]
                for f in range(2):
                    barj[f, k, at:at + 1, :] = rows_w[side, f, pl.ds(k, 1), :]
            for f in range(2):
                jp[f, k, before, :] = jhalo[0, f, pl.ds(k, 1), :]
                jp[f, k, after, :] = jhalo[1, f, pl.ds(k, 1), :]
            return c

        lax.fori_loop(0, radii, place, 0, unroll=4)

    rims_b = (rim_b, rtot_b, rpart_b, rslot_b)
    begin(0, sum_b, part_b, tot_b, slot_b, finish_edges, rims_b, ((0, 1), (cols - 2, cols - 1)))

    def local_step(k, carry):
        se, sa, sb, sja, sjb = carry
        beta = bp[k, inner]
        grow = jnp.exp((2.0 * step) * beta)
        es[k, inner] = grow
        dr[k, inner] = theta(beta)
        a, b = jp[0, k, inner], jp[1, k, inner]
        return (se + grow, sa + a, sb + b, sja + barj[0, k], sjb + barj[1, k])

    se, sa, sb, sja, sjb = lax.fori_loop(0, radii, local_step, (zero,) * 5, unroll=2)
    b_left.wait_recv()
    b_right.wait_recv()

    def halo_step(k, c):
        for i in range(2):
            bp[k, PAD - 2 + i:PAD - 1 + i, :] = bhalo[0, i, pl.ds(k, 1), :]
            bp[k, PAD + cols + i:PAD + cols + i + 1, :] = bhalo[1, i, pl.ds(k, 1), :]
        return c

    lax.fori_loop(0, radii, halo_step, 0, unroll=8)

    def halo_exp(k, c):
        for lo in (0, PAD + cols):
            x = bp[k, lo:lo + 8]
            es[k, lo:lo + 8] = jnp.exp((2.0 * step) * x)
            dr[k, lo:lo + 8] = theta(x)
        return c

    lax.fori_loop(0, radii, halo_exp, 0, unroll=4)
    bt[...] = jnp.zeros_like(bt)
    end(0, sum_b, part_b, tot_b, slot_b, below_b, rims_b)
    finish(0, sum_b, part_b, tot_b, slot_b, rims_b)
    bt[inner] = below_b[...]
    bt[PAD - 2:PAD] = rpart_b[0]
    bt[PAD + cols:PAD + cols + 2] = rpart_b[1]

    first = PAD - 1
    mid, hi, lo = slice(first, first + tall), slice(first + 1, first + tall + 1), slice(first - 1, first + tall - 1)
    base_r = theta(bt[mid])
    base_i = bt[hi] - bt[lo]
    base_g = step * jnp.exp((2.0 * step) * bt[mid])
    wide_zero = jnp.zeros((tall, lanes), f32)

    def u_step(k, carry):
        ua, ub = carry
        growth = base_g * es[k, mid]
        br = dr[k, mid] + base_r
        bi = 0.5 * ((bp[k, hi] - bp[k, lo]) + base_i)
        a, b = jp[0, k, mid], jp[1, k, mid]
        ua = ua + growth * (br - (a * br + b * bi))
        ub = ub + growth * (bi - (b * br - a * bi))
        up[0, k, mid] = ua
        up[1, k, mid] = ub
        return ua, ub

    ua_sum, ub_sum = lax.fori_loop(0, radii, u_step, (wide_zero, wide_zero), unroll=2)
    sum_u[:cols] = ua_sum[1:cols + 1]
    sum_u[cols:] = ub_sum[1:cols + 1]
    full_b = bt[inner]
    grow_b = jnp.exp((2.0 * step) * full_b)

    def wh_step(k, carry):
        sw, ha, hb = carry
        beta = bp[k, inner] + full_b
        growth = grow_b * es[k, inner]
        a, b = jp[0, k, inner], jp[1, k, inner]
        ua, ub = up[0, k, inner], up[1, k, inner]
        ta, tb = theta(ua), theta(ub)
        pa = 0.5 * (up[0, k, above] - up[0, k, below])
        pb = 0.5 * (up[1, k, above] - up[1, k, below])
        ja, jb = barj[0, k], barj[1, k]
        sw = sw + (growth * (ta + pb) + (b * ua - a * ub))
        ha = ha + ((ta - pb) + ua * ja - ub * jb + beta * a)
        hb = hb + ((tb + pa) + ua * jb + ub * ja + beta * b)
        cw[k] = sw
        ch[0, k] = ha
        ch[1, k] = hb
        return sw, ha, hb

    done = []
    ahead = radii // 4
    rims_u = (rim_u, rtot_u, rpart_u, rslot_u)
    begin(1, sum_u, part_u, tot_u, slot_u,
          lambda: done.extend(lax.fori_loop(0, ahead, wh_step, (zero, zero, zero))),
          rims_u, ((0, cols), (cols - 1, 2 * cols - 1)))
    sw, ha, hb = lax.fori_loop(ahead, radii, wh_step, tuple(done))
    end(1, sum_u, part_u, tot_u, slot_u, below_u, rims_u)
    finish(1, sum_u, part_u, tot_u, slot_u, rims_u)
    for f in range(2):
        ct[f] = jnp.zeros(ct.shape[1:], f32)
        ct[f, inner] = below_u[f * cols:(f + 1) * cols]
        ct[f, PAD - 1:PAD] = rpart_u[0, f:f + 1]
        ct[f, PAD + cols:PAD + cols + 1] = rpart_u[1, f:f + 1]
    ca, cb = ct[0, inner], ct[1, inner]
    re_bar, eth_a, eth_b = eth_planes(theta, ct, inner, above, below)
    n = float(radii)
    sum_h[:cols] = sw + (grow_b * se) * re_bar + (sb * ca - sa * cb)
    sum_h[cols:2 * cols] = ha + n * eth_a + (ca * sja - cb * sjb)
    sum_h[2 * cols:] = hb + n * eth_b + (ca * sjb + cb * sja)

    def fields_step(k, carry):
        dw, da, db = carry
        a, b = jp[0, k, inner], jp[1, k, inner]
        ja, jb = barj[0, k], barj[1, k]
        dw = dw + ((grow_b * es[k, inner]) * re_bar + (b * ca - a * cb))
        da = da + (eth_a + (ca * ja - cb * jb))
        db = db + (eth_b + (ca * jb + cb * ja))
        bfin[k] = step * (bp[k, inner] + full_b)
        ufin[0, k] = step * (up[0, k, inner] + ca)
        ufin[1, k] = step * (up[1, k, inner] + cb)
        cw[k] = cw[k] + dw
        ch[0, k] = ch[0, k] + da
        ch[1, k] = ch[1, k] + db
        return dw, da, db

    begin(2, sum_h, part_h, tot_h, slot_h, lambda: None)
    lax.fori_loop(0, radii, fields_step, (zero, zero, zero), unroll=2)
    end(2, sum_h, part_h, tot_h, slot_h, below_h)

    @pl.when(shell > 0)
    def _():
        down(shell - 1).wait_send()

    b_left.wait_send()
    b_right.wait_send()
    finish(2, sum_h, part_h, tot_h, slot_h)


def tail(step, bfin, ufin, cw, ch, below_h, beta_out, u_out, w_out, h_out, wv, hv, first_sems, sems):
    radii, cols, _ = cw.shape
    copies = [pltpu.make_async_copy(bfin, beta_out, first_sems.at[0]),
              pltpu.make_async_copy(ufin, u_out, first_sems.at[1])]
    for copy in copies:
        copy.start()
    w, ha, hb = (below_h[i * cols:(i + 1) * cols] for i in range(3))
    sq = step * step

    def final(k, c):
        wv[k] = sq * (cw[k] + w)
        hv[0, k] = sq * (ch[0, k] + ha)
        hv[1, k] = sq * (ch[1, k] + hb)
        return c

    chunks = sems.shape[0]
    size = radii // chunks
    for i in range(chunks):
        lax.fori_loop(i * size, (i + 1) * size, final, 0, unroll=4)
        at = pl.ds(i * size, size)
        more = [pltpu.make_async_copy(wv.at[at], w_out.at[at], sems.at[i, 0]),
                pltpu.make_async_copy(hv.at[:, at], h_out.at[:, at], sems.at[i, 1])]
        for copy in more:
            copy.start()
        copies += more
    for copy in copies:
        copy.wait()


def solution(mesh):
    shells, patches = mesh.shape["shell"], mesh.shape["patch"]
    chips = shells // 2

    def local(field_j):
        _, radii, cols, lanes = field_j.shape
        step = 1.0 / math.sqrt(radii * shells)
        f32 = jnp.float32
        vm = lambda *s: pltpu.VMEM(s, f32)
        shape = lambda *s: jax.ShapeDtypeStruct(s, f32)
        tall = cols + 2 * PAD
        dma = pltpu.SemaphoreType.DMA
        vmem = pl.BlockSpec(memory_space=pltpu.VMEM)
        hbm = pl.BlockSpec(memory_space=pltpu.HBM)
        plain, pair = (radii, cols, lanes), (2, radii, cols, lanes)
        padded = (2, radii, tall, lanes)
        limit = 24 * 1024 * 1024
        many = max(chips - 1, 1)
        regular = pltpu.SemaphoreType.REGULAR
        planes = vm(2, 2, radii, lanes)
        scratch = [vm(*padded), vm(*pair), vm(*padded), vm(2, tall, lanes)]
        scratch += [vm(radii, tall, lanes)] * 3 + [vm(tall, lanes), planes, planes, vm(cols, lanes), vm(2 * cols, lanes),
                                                  vm(2, cols, lanes), vm(2, 2, radii + 8, lanes), planes, planes, planes]
        for n in (1, 2, 3):
            scratch += [vm(n * cols, lanes)] * 3 + [vm(many, n * cols, lanes)]
        for _ in range(2):
            scratch += [vm(2, 2, lanes)] * 3 + [vm(many, 2, 2, lanes)]
        scratch += [dma, dma((2,)), dma((2,)), dma((2,)), regular, regular,
                    dma((2,)), dma, dma((3,)), dma((many, 2)), dma((3, many, 2)),
                    dma((2,)), dma((2, 2)), dma((many, 2)), dma((2, many, 2))]
        found = pl.pallas_call(
            functools.partial(kernel, shells, patches, step),
            out_shape=(shape(*plain), shape(*pair), shape(*plain), shape(*pair), shape(3 * cols, lanes)),
            in_specs=[hbm],
            out_specs=(vmem,) * 5,
            scratch_shapes=scratch,
            compiler_params=pltpu.CompilerParams(
                collective_id=0, has_side_effects=True, vmem_limit_bytes=limit),
        )(pltpu.with_memory_space_constraint(field_j, pltpu.HBM))
        return pl.pallas_call(
            functools.partial(tail, step),
            out_shape=(shape(*plain), shape(*pair), shape(*plain), shape(*pair)),
            in_specs=[vmem] * 5,
            out_specs=(hbm,) * 4,
            scratch_shapes=[vm(*plain), vm(*pair), dma((2,)), dma((2, 2))],
            compiler_params=pltpu.CompilerParams(vmem_limit_bytes=limit),
        )(*found)

    return jax.shard_map(
        local,
        mesh=mesh,
        in_specs=(P(None, "shell", "patch", None),),
        out_specs=(
            P("shell", "patch", None),
            P(None, "shell", "patch", None),
            P("shell", "patch", None),
            P(None, "shell", "patch", None),
        ),
        check_vma=False,
    )
```

```python
import functools
import math

import jax
import jax.numpy as jnp
from jax import lax
from jax.experimental import pallas as pl
from jax.experimental.pallas import tpu as pltpu
from jax.sharding import PartitionSpec as P

PAD = 8


def remote(src, dst, send_sem, recv_sem, shell, patch):
    return pltpu.make_async_remote_copy(
        src_ref=src,
        dst_ref=dst,
        send_sem=send_sem,
        recv_sem=recv_sem,
        device_id=(shell, patch),
        device_id_type=pl.DeviceIdType.MESH,
    )


def make_theta(lanes):
    lane = lax.broadcasted_iota(jnp.int32, (8, lanes), 1)
    keep_f = jnp.where(lane == lanes - 1, 0.0, 0.5).astype(jnp.float32)
    keep_b = jnp.where(lane == 0, 0.0, 0.5).astype(jnp.float32)

    def theta(x):
        reps = x.shape[0] // 8
        mf = jnp.concatenate([keep_f] * reps, axis=0) if reps > 1 else keep_f
        mb = jnp.concatenate([keep_b] * reps, axis=0) if reps > 1 else keep_b
        return pltpu.roll(x, lanes - 1, 1) * mf - pltpu.roll(x, 1, 1) * mb

    return theta


def eth_planes(theta, pair, inner, above, below):
    ta, tb = theta(pair[0, inner]), theta(pair[1, inner])
    pa = 0.5 * (pair[0, above] - pair[0, below])
    pb = 0.5 * (pair[1, above] - pair[1, below])
    return ta + pb, ta - pb, tb + pa


def beta_terms(theta, a, b, next_a, next_b, pa, pb):
    ra, rb = next_a - a, next_b - b
    ta, tb = theta(a), theta(b)
    ea, eb = ta - pb, tb + pa
    return 0.25 * (0.5 * (ra * ra + rb * rb) - (ea * ea + eb * eb)), ta + pb, tb - pa


def kernel(shells, patches, step, j_hbm, bfin, ufin, cw, ch, below_h,
           jp, barj, up, ct, bp, es, dr, bt, bedge, bhalo, below_b, below_u, jnext, jedge, jside, jhalo, rows_w,
           sum_b, part_b, tot_b, slot_b,
           sum_u, part_u, tot_u, slot_u, pre_u,
           sum_h, part_h, tot_h, slot_h, pre_h,
           rim_b, rtot_b, rpart_b, rslot_b, rim_u, rtot_u, rpart_u, rslot_u,
           load_sem, rad_sem, jh_send, jh_recv, next_ready, up_ready, side_ready,
           edge_recv, part_send, part_recv, send_sem, recv_sem, fwd_send, fwd_recv,
           rpart_send, rpart_recv, rim_send, rim_recv):
    radii, cols, lanes = cw.shape
    tall = cols + 8
    f32 = jnp.float32
    chips = shells // 2
    shell, patch = lax.axis_index("shell"), lax.axis_index("patch")
    chip, core = shell // 2, shell % 2
    partner = shell + 1 - 2 * core
    right = lax.rem(patch + 1, patches)
    left = lax.rem(patch + patches - 1, patches)
    inner = slice(PAD, PAD + cols)
    above = slice(PAD + 1, PAD + cols + 1)
    below = slice(PAD - 1, PAD + cols - 1)
    before, after = slice(PAD - 1, PAD), slice(PAD + cols, PAD + cols + 1)
    theta = make_theta(lanes)
    mesh_id = pl.DeviceIdType.MESH

    load = pltpu.make_async_copy(j_hbm, jp.at[:, :, pl.ds(PAD, cols), :], load_sem)
    load.start()

    barrier = pltpu.get_barrier_semaphore()
    def greet(there, p):
        pl.semaphore_signal(barrier, inc=1, device_id=(there, p), device_id_type=mesh_id)

    greet(partner, patch)
    greet(shell, left)
    greet(shell, right)

    @pl.when(chip > 0)
    def _():
        greet(shell - 2, patch)

        @pl.when(chip > 1)
        def _():
            greet(shell - 4, patch)

        @pl.when(core == 0)
        def _():
            greet(shell - 1, patch)

    @pl.when(chip < chips - 1)
    def _():
        greet(shell + 2, patch)

        @pl.when(chip < chips - 2)
        def _():
            greet(shell + 4, patch)

        @pl.when(core == 1)
        def _():
            greet(shell + 1, patch)

    load.wait()

    def pack(k, c):
        for f in range(2):
            jedge[0, f, pl.ds(k, 1), :] = jp[f, k, PAD:PAD + 1, :]
            jedge[1, f, pl.ds(k, 1), :] = jp[f, k, PAD + cols - 1:PAD + cols, :]
        return c

    lax.fori_loop(0, radii, pack, 0, unroll=8)
    inside, outside = (chip > 0).astype(jnp.int32), (chip < chips - 1).astype(jnp.int32)
    further = (chip > 1).astype(jnp.int32) + (chip < chips - 2).astype(jnp.int32)
    pl.semaphore_wait(barrier, 3 + inside * (2 - core) + outside * (1 + core) + further)
    to_left = remote(jedge.at[0, :, pl.ds(0, radii)], jhalo.at[1], jh_send.at[0], jh_recv.at[1], shell, left)
    to_right = remote(jedge.at[1, :, pl.ds(0, radii)], jhalo.at[0], jh_send.at[1], jh_recv.at[0], shell, right)
    to_left.start()
    to_right.start()

    @pl.when(chip > 0)
    def _():
        pl.semaphore_signal(next_ready, inc=1, device_id=(shell - 2, patch), device_id_type=mesh_id)

    def chain(step_at):
        @pl.when(step_at)
        def _():
            @pl.when(chip < chips - 1)
            def _():
                pl.semaphore_wait(next_ready, 1)

            @pl.when(chip < chips - 2)
            def _():
                pl.semaphore_wait(up_ready, 1)

            @pl.when(chip > 1)
            def _():
                pl.semaphore_signal(up_ready, inc=1, device_id=(shell - 4, patch), device_id_type=mesh_id)

            pl.semaphore_signal(side_ready, inc=1, device_id=(partner, patch), device_id_type=mesh_id)

    chain(chip == chips - 1)

    def down(there):
        return remote(j_hbm.at[:, 0], jnext, rad_sem.at[0], rad_sem.at[1], there, patch)

    @pl.when(shell > 0)
    def _():
        down(shell - 1).start()

    def pack_side(k, c):
        for f in range(2):
            jside[0, f, pl.ds(k, 1), :] = jp[f, k, PAD + 1:PAD + 2, :]
            jside[1, f, pl.ds(k, 1), :] = jp[f, k, PAD + cols - 2:PAD + cols - 1, :]
        return c

    lax.fori_loop(0, radii, pack_side, 0, unroll=8)

    def beta_step(k, next_a, next_b, total):
        pa = 0.5 * (jp[0, k, above] - jp[0, k, below])
        pb = 0.5 * (jp[1, k, above] - jp[1, k, below])
        source, ja, jb = beta_terms(theta, jp[0, k, inner], jp[1, k, inner], next_a, next_b, pa, pb)
        barj[0, k], barj[1, k] = ja, jb
        total = total + source
        bp[k, inner] = total
        bedge[0, 1, pl.ds(k, 1), :] = total[1:2]
        bedge[1, 0, pl.ds(k, 1), :] = total[cols - 2:cols - 1]
        return total

    zero = jnp.zeros((cols, lanes), f32)
    total = zero
    slices = 4
    for i in range(slices):
        stop = (i + 1) * radii // slices if i < slices - 1 else radii - 1
        total = lax.fori_loop(
            i * radii // slices, stop,
            lambda k, t: beta_step(k, jp[0, k + 1, inner], jp[1, k + 1, inner], t), total, unroll=2)
        if i == slices // 2 - 1 and chips > 1:
            chain(chip == chips - 2)

    @pl.when(shell == shells - 1)
    def _():
        for f in range(2):
            jnext[f] = jp[f, radii - 1, inner]

    @pl.when(shell < shells - 1)
    def _():
        down(shell).wait_recv()

    sum_b[...] = beta_step(radii - 1, jnext[0], jnext[1], total)
    for f in range(2):
        jedge[0, f, radii:radii + 1] = jnext[f, 0:1]
        jedge[1, f, radii:radii + 1] = jnext[f, cols - 1:cols]
    for c in range(chips - 3, 0, -1):
        chain(chip == c)
    to_left.wait_recv()
    to_right.wait_recv()
    to_left.wait_send()
    to_right.wait_send()
    edge_sources = []
    for side, (over, under) in enumerate(((jside.at[0], jhalo.at[0]), (jhalo.at[1], jside.at[1]))):
        pa, pb = (0.5 * (over[f] - under[f]) for f in range(2))
        source, ja, jb = beta_terms(
            theta, jedge[side, 0, 0:radii], jedge[side, 1, 0:radii],
            jedge[side, 0, 1:radii + 1], jedge[side, 1, 1:radii + 1], pa, pb)
        rows_w[side, 0], rows_w[side, 1] = ja, jb
        edge_sources.append(source)
        at = side * (cols - 1)
        sum_b[at:at + 1] = jnp.sum(source, axis=0, keepdims=True)

    def pieces(stage, own, part, tot, slots):
        half = own.shape[0] // 2
        mine = pl.ds(pl.multiple_of(core * half, 8), half)
        first = remote(own, part, part_send, part_recv.at[stage], partner, patch)
        sends = []
        for d in range(1, chips):
            if stage == 0:
                sends.append([
                    remote(tot.at[mine], slots.at[d - 1, mine], send_sem.at[d - 1, e],
                           recv_sem.at[d - 1, core], (chip + d) * 2 + e, patch)
                    for e in range(2)])
            else:
                sends.append([
                    remote(tot.at[mine], slots.at[d - 1, mine], send_sem.at[d - 1, 0],
                           recv_sem.at[d - 1, 1 + stage], (chip + d) * 2 + core, patch)])
        return mine, half, first, sends

    def forward(stage, pre, mine):
        return remote(pre.at[mine], pre.at[mine], fwd_send, fwd_recv.at[stage - 1], partner, patch)

    def rim_pieces(stage, rim, rtot, rpart, rslot):
        over = left * (1 - core) + right * core
        near = [
            remote(rim.at[0], rpart.at[1], rpart_send.at[0], rpart_recv.at[stage, 1], partner, left),
            remote(rim.at[1], rpart.at[0], rpart_send.at[1], rpart_recv.at[stage, 0], partner, right)]
        far = [[
            remote(rtot.at[core], rslot.at[d - 1, 1 - core], rim_send.at[d - 1, e],
                   rim_recv.at[stage, d - 1, 1 - core], (chip + d) * 2 + e, over)
            for e in range(2)] for d in range(1, chips)]
        return near, far

    def begin(stage, own, part, tot, slots, during, rims=None, lines=None):
        mine, half, first, sends = pieces(stage, own, part, tot, slots)
        first.start()
        if rims is not None:
            rim, rtot, rpart, rslot = rims
            for side in range(2):
                for i, r in enumerate(lines[side]):
                    rim[side, i:i + 1] = own[r:r + 1]
            near, far = rim_pieces(stage, rim, rtot, rpart, rslot)

            @pl.when(core == 0)
            def _():
                for copy in near:
                    copy.start()

        during()
        first.wait_recv()
        tot[mine] = own[mine] + part[mine]
        if rims is not None:
            for side in range(2):
                for i, r in enumerate(lines[side]):
                    rtot[side, i:i + 1] = own[r:r + 1] + part[r:r + 1]
        for d in range(chips - 1, 0, -1):
            @pl.when(chip + d < chips)
            def _():
                for copy in sends[d - 1]:
                    copy.start()
                if rims is not None:
                    for copy in far[d - 1]:
                        copy.start()

    def end(stage, own, part, tot, slots, out, rims=None, pre=None):
        mine, half, first, sends = pieces(stage, own, part, tot, slots)
        if rims is not None:
            rim, rtot, rpart, rslot = rims
            near, far = rim_pieces(stage, rim, rtot, rpart, rslot)

        @pl.when(core == 0)
        def _():
            out[...] = jnp.zeros_like(out)

        @pl.when(core == 1)
        def _():
            out[...] = part[...]
            if rims is not None:
                for copy in near:
                    copy.wait_recv()

        if rims is not None:
            @pl.when(core == 0)
            def _():
                rpart[...] = jnp.zeros_like(rpart)

        if stage == 0:
            for d in range(1, chips):
                @pl.when(chip >= d)
                def _():
                    for e in range(2):
                        piece = pl.ds(e * half, half)
                        remote(tot.at[piece], slots.at[d - 1, piece], send_sem.at[d - 1, e],
                               recv_sem.at[d - 1, e], shell, patch).wait_recv()
                    out[...] += slots[d - 1]
        else:
            @pl.when(chip > 0)
            def _():
                pre[mine] = jnp.zeros((half, lanes), f32)

            for d in range(1, chips):
                @pl.when(chip >= d)
                def _():
                    for copy in sends[d - 1]:
                        copy.wait_recv()
                    pre[mine] += slots[d - 1, mine]

            @pl.when(chip > 0)
            def _():
                fwd = forward(stage, pre, mine)
                fwd.start()
                fwd.wait_recv()
                out[...] += pre[...]

        if rims is not None:
            for d in range(1, chips):
                @pl.when(chip >= d)
                def _():
                    for e in range(2):
                        remote(rtot.at[e], rslot.at[d - 1, e], rim_send.at[d - 1, 0],
                               rim_recv.at[stage, d - 1, e], shell, patch).wait_recv()
                    rpart[...] += rslot[d - 1]

    def finish(stage, own, part, tot, slots, rims=None, pre=None):
        mine, half, first, sends = pieces(stage, own, part, tot, slots)
        first.wait_send()
        if rims is not None:
            near, far = rim_pieces(stage, *rims)

            @pl.when(core == 0)
            def _():
                for copy in near:
                    copy.wait_send()

        for d in range(1, chips):
            @pl.when(chip + d < chips)
            def _():
                for copy in sends[d - 1]:
                    copy.wait_send()
                if rims is not None:
                    for copy in far[d - 1]:
                        copy.wait_send()

        if stage > 0:
            @pl.when(chip > 0)
            def _():
                forward(stage, pre, mine).wait_send()

    if chips > 2:
        chain(chip == 0)
    pl.semaphore_wait(side_ready, 1)
    b_left = remote(bedge.at[0], bhalo.at[1], jh_send.at[0], edge_recv.at[1], shell, left)
    b_right = remote(bedge.at[1], bhalo.at[0], jh_send.at[1], edge_recv.at[0], shell, right)

    def finish_edges():
        row = lax.broadcasted_iota(jnp.int32, (radii, lanes), 0)
        for side in range(2):
            x, shift = edge_sources[side], 1
            while shift < radii:
                x = x + jnp.where(row >= shift, pltpu.roll(x, shift, 0), 0.0)
                shift *= 2
            bedge[side, side] = x
        b_left.start()
        b_right.start()

        def place(k, c):
            for side in range(2):
                at = side * (cols - 1)
                bp[k, PAD + at:PAD + at + 1, :] = bedge[side, side, pl.ds(k, 1), :]
                for f in range(2):
                    barj[f, k, at:at + 1, :] = rows_w[side, f, pl.ds(k, 1), :]
            for f in range(2):
                jp[f, k, before, :] = jhalo[0, f, pl.ds(k, 1), :]
                jp[f, k, after, :] = jhalo[1, f, pl.ds(k, 1), :]
            return c

        lax.fori_loop(0, radii, place, 0, unroll=4)

    rims_b = (rim_b, rtot_b, rpart_b, rslot_b)
    begin(0, sum_b, part_b, tot_b, slot_b, finish_edges, rims_b, ((0, 1), (cols - 2, cols - 1)))

    def local_step(k, carry):
        se, sa, sb, sja, sjb = carry
        beta = bp[k, inner]
        grow = jnp.exp((2.0 * step) * beta)
        es[k, inner] = grow
        dr[k, inner] = theta(beta)
        a, b = jp[0, k, inner], jp[1, k, inner]
        return (se + grow, sa + a, sb + b, sja + barj[0, k], sjb + barj[1, k])

    se, sa, sb, sja, sjb = lax.fori_loop(0, radii, local_step, (zero,) * 5, unroll=2)
    b_left.wait_recv()
    b_right.wait_recv()

    for side in range(2):
        x = bhalo[side, 1 - side]
        rows_w[side, 0] = jnp.exp((2.0 * step) * x)
        rows_w[side, 1] = theta(x)

    def halo_step(k, c):
        for i in range(2):
            bp[k, PAD - 2 + i:PAD - 1 + i, :] = bhalo[0, i, pl.ds(k, 1), :]
            bp[k, PAD + cols + i:PAD + cols + i + 1, :] = bhalo[1, i, pl.ds(k, 1), :]
        for side, at in enumerate((before, after)):
            es[k, at, :] = rows_w[side, 0, pl.ds(k, 1), :]
            dr[k, at, :] = rows_w[side, 1, pl.ds(k, 1), :]
        return c

    lax.fori_loop(0, radii, halo_step, 0, unroll=4)
    bt[...] = jnp.zeros_like(bt)
    end(0, sum_b, part_b, tot_b, slot_b, below_b, rims_b)
    finish(0, sum_b, part_b, tot_b, slot_b, rims_b)
    bt[inner] = below_b[...]
    bt[PAD - 2:PAD] = rpart_b[0]
    bt[PAD + cols:PAD + cols + 2] = rpart_b[1]

    first = PAD - 1
    mid, hi, lo = slice(first, first + tall), slice(first + 1, first + tall + 1), slice(first - 1, first + tall - 1)
    base_r = theta(bt[mid])
    base_i = bt[hi] - bt[lo]
    base_g = step * jnp.exp((2.0 * step) * bt[mid])
    wide_zero = jnp.zeros((tall, lanes), f32)

    def u_step(k, carry):
        ua, ub = carry
        growth = base_g * es[k, mid]
        br = dr[k, mid] + base_r
        bi = 0.5 * ((bp[k, hi] - bp[k, lo]) + base_i)
        a, b = jp[0, k, mid], jp[1, k, mid]
        ua = ua + growth * (br - (a * br + b * bi))
        ub = ub + growth * (bi - (b * br - a * bi))
        up[0, k, mid] = ua
        up[1, k, mid] = ub
        return ua, ub

    ua_sum, ub_sum = lax.fori_loop(0, radii, u_step, (wide_zero, wide_zero), unroll=2)
    sum_u[:cols] = ua_sum[1:cols + 1]
    sum_u[cols:] = ub_sum[1:cols + 1]
    full_b = bt[inner]
    grow_b = jnp.exp((2.0 * step) * full_b)

    def wh_step(k, carry):
        sw, ha, hb = carry
        beta = bp[k, inner] + full_b
        growth = grow_b * es[k, inner]
        a, b = jp[0, k, inner], jp[1, k, inner]
        ua, ub = up[0, k, inner], up[1, k, inner]
        ta, tb = theta(ua), theta(ub)
        pa = 0.5 * (up[0, k, above] - up[0, k, below])
        pb = 0.5 * (up[1, k, above] - up[1, k, below])
        ja, jb = barj[0, k], barj[1, k]
        sw = sw + (growth * (ta + pb) + (b * ua - a * ub))
        ha = ha + ((ta - pb) + ua * ja - ub * jb + beta * a)
        hb = hb + ((tb + pa) + ua * jb + ub * ja + beta * b)
        cw[k] = sw
        ch[0, k] = ha
        ch[1, k] = hb
        return sw, ha, hb

    done = []
    ahead = radii // 4
    rims_u = (rim_u, rtot_u, rpart_u, rslot_u)
    begin(1, sum_u, part_u, tot_u, slot_u,
          lambda: done.extend(lax.fori_loop(0, ahead, wh_step, (zero, zero, zero))),
          rims_u, ((0, cols), (cols - 1, 2 * cols - 1)))
    sw, ha, hb = lax.fori_loop(ahead, radii, wh_step, tuple(done))
    end(1, sum_u, part_u, tot_u, slot_u, below_u, rims_u, pre_u)
    finish(1, sum_u, part_u, tot_u, slot_u, rims_u, pre_u)
    for f in range(2):
        ct[f] = jnp.zeros(ct.shape[1:], f32)
        ct[f, inner] = below_u[f * cols:(f + 1) * cols]
        ct[f, PAD - 1:PAD] = rpart_u[0, f:f + 1]
        ct[f, PAD + cols:PAD + cols + 1] = rpart_u[1, f:f + 1]
    ca, cb = ct[0, inner], ct[1, inner]
    re_bar, eth_a, eth_b = eth_planes(theta, ct, inner, above, below)
    n = float(radii)
    sum_h[:cols] = sw + (grow_b * se) * re_bar + (sb * ca - sa * cb)
    sum_h[cols:2 * cols] = ha + n * eth_a + (ca * sja - cb * sjb)
    sum_h[2 * cols:] = hb + n * eth_b + (ca * sjb + cb * sja)

    def fields_step(k, carry):
        dw, da, db = carry
        a, b = jp[0, k, inner], jp[1, k, inner]
        ja, jb = barj[0, k], barj[1, k]
        dw = dw + ((grow_b * es[k, inner]) * re_bar + (b * ca - a * cb))
        da = da + (eth_a + (ca * ja - cb * jb))
        db = db + (eth_b + (ca * jb + cb * ja))
        bfin[k] = step * (bp[k, inner] + full_b)
        ufin[0, k] = step * (up[0, k, inner] + ca)
        ufin[1, k] = step * (up[1, k, inner] + cb)
        cw[k] = cw[k] + dw
        ch[0, k] = ch[0, k] + da
        ch[1, k] = ch[1, k] + db
        return dw, da, db

    begin(2, sum_h, part_h, tot_h, slot_h, lambda: None)
    lax.fori_loop(0, radii, fields_step, (zero, zero, zero), unroll=2)
    end(2, sum_h, part_h, tot_h, slot_h, below_h, None, pre_h)

    @pl.when(shell > 0)
    def _():
        down(shell - 1).wait_send()

    b_left.wait_send()
    b_right.wait_send()
    finish(2, sum_h, part_h, tot_h, slot_h, None, pre_h)


def tail(step, bfin, ufin, cw, ch, below_h, beta_out, u_out, w_out, h_out, wv, hv, first_sems, sems):
    radii, cols, _ = cw.shape
    copies = [pltpu.make_async_copy(bfin, beta_out, first_sems.at[0]),
              pltpu.make_async_copy(ufin, u_out, first_sems.at[1])]
    for copy in copies:
        copy.start()
    w, ha, hb = (below_h[i * cols:(i + 1) * cols] for i in range(3))
    sq = step * step

    def final(k, c):
        wv[k] = sq * (cw[k] + w)
        hv[0, k] = sq * (ch[0, k] + ha)
        hv[1, k] = sq * (ch[1, k] + hb)
        return c

    chunks = sems.shape[0]
    size = radii // chunks
    for i in range(chunks):
        lax.fori_loop(i * size, (i + 1) * size, final, 0, unroll=4)
        at = pl.ds(i * size, size)
        more = [pltpu.make_async_copy(wv.at[at], w_out.at[at], sems.at[i, 0]),
                pltpu.make_async_copy(hv.at[:, at], h_out.at[:, at], sems.at[i, 1])]
        for copy in more:
            copy.start()
        copies += more
    for copy in copies:
        copy.wait()


def solution(mesh):
    shells, patches = mesh.shape["shell"], mesh.shape["patch"]
    chips = shells // 2

    def local(field_j):
        _, radii, cols, lanes = field_j.shape
        step = 1.0 / math.sqrt(radii * shells)
        f32 = jnp.float32
        vm = lambda *s: pltpu.VMEM(s, f32)
        shape = lambda *s: jax.ShapeDtypeStruct(s, f32)
        tall = cols + 2 * PAD
        dma = pltpu.SemaphoreType.DMA
        vmem = pl.BlockSpec(memory_space=pltpu.VMEM)
        hbm = pl.BlockSpec(memory_space=pltpu.HBM)
        plain, pair = (radii, cols, lanes), (2, radii, cols, lanes)
        padded = (2, radii, tall, lanes)
        limit = 24 * 1024 * 1024
        many = max(chips - 1, 1)
        regular = pltpu.SemaphoreType.REGULAR
        planes = vm(2, 2, radii, lanes)
        scratch = [vm(*padded), vm(*pair), vm(*padded), vm(2, tall, lanes)]
        scratch += [vm(radii, tall, lanes)] * 3 + [vm(tall, lanes), planes, planes, vm(cols, lanes), vm(2 * cols, lanes),
                                                  vm(2, cols, lanes), vm(2, 2, radii + 8, lanes), planes, planes, planes]
        for n in (1, 2, 3):
            scratch += [vm(n * cols, lanes)] * 3 + [vm(many, n * cols, lanes)] + [vm(n * cols, lanes)] * (n > 1)
        for _ in range(2):
            scratch += [vm(2, 2, lanes)] * 3 + [vm(many, 2, 2, lanes)]
        scratch += [dma, dma((2,)), dma((2,)), dma((2,)), regular, regular, regular,
                    dma((2,)), dma, dma((3,)), dma((many, 2)), dma((many, 4)), dma, dma((2,)),
                    dma((2,)), dma((2, 2)), dma((many, 2)), dma((2, many, 2))]
        found = pl.pallas_call(
            functools.partial(kernel, shells, patches, step),
            out_shape=(shape(*plain), shape(*pair), shape(*plain), shape(*pair), shape(3 * cols, lanes)),
            in_specs=[hbm],
            out_specs=(vmem,) * 5,
            scratch_shapes=scratch,
            compiler_params=pltpu.CompilerParams(
                collective_id=0, has_side_effects=True, vmem_limit_bytes=limit),
        )(pltpu.with_memory_space_constraint(field_j, pltpu.HBM))
        return pl.pallas_call(
            functools.partial(tail, step),
            out_shape=(shape(*plain), shape(*pair), shape(*plain), shape(*pair)),
            in_specs=[vmem] * 5,
            out_specs=(hbm,) * 4,
            scratch_shapes=[vm(*plain), vm(*pair), dma((2,)), dma((2, 2))],
            compiler_params=pltpu.CompilerParams(vmem_limit_bytes=limit),
        )(*found)

    return jax.shard_map(
        local,
        mesh=mesh,
        in_specs=(P(None, "shell", "patch", None),),
        out_specs=(
            P("shell", "patch", None),
            P(None, "shell", "patch", None),
            P("shell", "patch", None),
            P(None, "shell", "patch", None),
        ),
        check_vma=False,
    )
```

```python
import functools
import math

import jax
import jax.numpy as jnp
from jax import lax
from jax.experimental import pallas as pl
from jax.experimental.pallas import tpu as pltpu
from jax.sharding import PartitionSpec as P

PAD = 8


def remote(src, dst, send_sem, recv_sem, shell, patch):
    return pltpu.make_async_remote_copy(
        src_ref=src,
        dst_ref=dst,
        send_sem=send_sem,
        recv_sem=recv_sem,
        device_id=(shell, patch),
        device_id_type=pl.DeviceIdType.MESH,
    )


def make_theta(lanes):
    lane = lax.broadcasted_iota(jnp.int32, (8, lanes), 1)
    keep_f = jnp.where(lane == lanes - 1, 0.0, 0.5).astype(jnp.float32)
    keep_b = jnp.where(lane == 0, 0.0, 0.5).astype(jnp.float32)

    def theta(x):
        reps = x.shape[0] // 8
        mf = jnp.concatenate([keep_f] * reps, axis=0) if reps > 1 else keep_f
        mb = jnp.concatenate([keep_b] * reps, axis=0) if reps > 1 else keep_b
        return pltpu.roll(x, lanes - 1, 1) * mf - pltpu.roll(x, 1, 1) * mb

    return theta


def eth_planes(theta, pair, inner, above, below):
    ta, tb = theta(pair[0, inner]), theta(pair[1, inner])
    pa = 0.5 * (pair[0, above] - pair[0, below])
    pb = 0.5 * (pair[1, above] - pair[1, below])
    return ta + pb, ta - pb, tb + pa


def beta_terms(theta, a, b, next_a, next_b, pa, pb):
    ra, rb = next_a - a, next_b - b
    ta, tb = theta(a), theta(b)
    ea, eb = ta - pb, tb + pa
    return 0.25 * (0.5 * (ra * ra + rb * rb) - (ea * ea + eb * eb)), ta + pb, tb - pa


def kernel(shells, patches, step, j_hbm, bfin, ufin, cw, ch, below_h,
           jp, barj, up, ct, bp, es, dr, bt, bedge, bhalo, below_b, below_u, jnext, jedge, jside, jhalo, rows_w,
           sum_b, part_b, tot_b, slot_b,
           sum_u, part_u, tot_u, slot_u, pre_u,
           sum_h, part_h, tot_h, slot_h, pre_h,
           rim_b, rtot_b, rpart_b, rslot_b, rim_u, rtot_u, rpart_u, rslot_u,
           load_sem, rad_sem, jh_send, jh_recv, next_ready, up_ready, side_ready,
           edge_recv, part_send, part_recv, send_sem, recv_sem, fwd_send, fwd_recv,
           rpart_send, rpart_recv, rim_send, rim_recv):
    radii, cols, lanes = cw.shape
    tall = cols + 8
    f32 = jnp.float32
    chips = shells // 2
    shell, patch = lax.axis_index("shell"), lax.axis_index("patch")
    chip, core = shell // 2, shell % 2
    partner = shell + 1 - 2 * core
    right = lax.rem(patch + 1, patches)
    left = lax.rem(patch + patches - 1, patches)
    inner = slice(PAD, PAD + cols)
    above = slice(PAD + 1, PAD + cols + 1)
    below = slice(PAD - 1, PAD + cols - 1)
    before, after = slice(PAD - 1, PAD), slice(PAD + cols, PAD + cols + 1)
    theta = make_theta(lanes)
    mesh_id = pl.DeviceIdType.MESH

    load = pltpu.make_async_copy(j_hbm, jp.at[:, :, pl.ds(PAD, cols), :], load_sem)
    load.start()

    barrier = pltpu.get_barrier_semaphore()
    def greet(there, p):
        pl.semaphore_signal(barrier, inc=1, device_id=(there, p), device_id_type=mesh_id)

    greet(partner, patch)
    greet(shell, left)
    greet(shell, right)

    @pl.when(chip < chips - 1)
    def _():
        greet(shell + 2, patch)

        @pl.when(chip < chips - 2)
        def _():
            greet(shell + 4, patch)

        @pl.when(core == 1)
        def _():
            greet(shell + 1, patch)

    load.wait()

    def pack(k, c):
        for f in range(2):
            jedge[0, f, pl.ds(k, 1), :] = jp[f, k, PAD:PAD + 1, :]
            jedge[1, f, pl.ds(k, 1), :] = jp[f, k, PAD + cols - 1:PAD + cols, :]
        return c

    lax.fori_loop(0, radii, pack, 0, unroll=8)
    inside, second = (chip > 0).astype(jnp.int32), (chip > 1).astype(jnp.int32)
    pl.semaphore_wait(barrier, 3 + inside * (2 - core) + second)
    to_left = remote(jedge.at[0, :, pl.ds(0, radii)], jhalo.at[1], jh_send.at[0], jh_recv.at[1], shell, left)
    to_right = remote(jedge.at[1, :, pl.ds(0, radii)], jhalo.at[0], jh_send.at[1], jh_recv.at[0], shell, right)
    to_left.start()
    to_right.start()

    @pl.when(chip > 0)
    def _():
        pl.semaphore_signal(next_ready, inc=1, device_id=(shell - 2, patch), device_id_type=mesh_id)

    def chain(step_at):
        @pl.when(step_at)
        def _():
            @pl.when(chip < chips - 1)
            def _():
                pl.semaphore_wait(next_ready, 1)

            @pl.when(chip < chips - 2)
            def _():
                pl.semaphore_wait(up_ready, 1)

            @pl.when(chip > 1)
            def _():
                pl.semaphore_signal(up_ready, inc=1, device_id=(shell - 4, patch), device_id_type=mesh_id)

            pl.semaphore_signal(side_ready, inc=1, device_id=(partner, patch), device_id_type=mesh_id)

    chain(chip == chips - 1)

    def down(there):
        return remote(j_hbm.at[:, 0], jnext, rad_sem.at[0], rad_sem.at[1], there, patch)

    @pl.when(shell > 0)
    def _():
        down(shell - 1).start()

    def pack_side(k, c):
        for f in range(2):
            jside[0, f, pl.ds(k, 1), :] = jp[f, k, PAD + 1:PAD + 2, :]
            jside[1, f, pl.ds(k, 1), :] = jp[f, k, PAD + cols - 2:PAD + cols - 1, :]
        return c

    lax.fori_loop(0, radii, pack_side, 0, unroll=8)

    def beta_step(k, next_a, next_b, total):
        pa = 0.5 * (jp[0, k, above] - jp[0, k, below])
        pb = 0.5 * (jp[1, k, above] - jp[1, k, below])
        source, ja, jb = beta_terms(theta, jp[0, k, inner], jp[1, k, inner], next_a, next_b, pa, pb)
        barj[0, k], barj[1, k] = ja, jb
        total = total + source
        bp[k, inner] = total
        bedge[0, 1, pl.ds(k, 1), :] = total[1:2]
        bedge[1, 0, pl.ds(k, 1), :] = total[cols - 2:cols - 1]
        return total

    zero = jnp.zeros((cols, lanes), f32)
    total = zero
    slices = 4
    for i in range(slices):
        stop = (i + 1) * radii // slices if i < slices - 1 else radii - 1
        total = lax.fori_loop(
            i * radii // slices, stop,
            lambda k, t: beta_step(k, jp[0, k + 1, inner], jp[1, k + 1, inner], t), total, unroll=2)
        if i == slices // 2 - 1 and chips > 1:
            chain(chip == chips - 2)

    @pl.when(shell == shells - 1)
    def _():
        for f in range(2):
            jnext[f] = jp[f, radii - 1, inner]

    @pl.when(shell < shells - 1)
    def _():
        down(shell).wait_recv()

    sum_b[...] = beta_step(radii - 1, jnext[0], jnext[1], total)
    for f in range(2):
        jedge[0, f, radii:radii + 1] = jnext[f, 0:1]
        jedge[1, f, radii:radii + 1] = jnext[f, cols - 1:cols]
    for c in range(chips - 3, 0, -1):
        chain(chip == c)
    to_left.wait_recv()
    to_right.wait_recv()
    to_left.wait_send()
    to_right.wait_send()
    edge_sources = []
    for side, (over, under) in enumerate(((jside.at[0], jhalo.at[0]), (jhalo.at[1], jside.at[1]))):
        pa, pb = (0.5 * (over[f] - under[f]) for f in range(2))
        source, ja, jb = beta_terms(
            theta, jedge[side, 0, 0:radii], jedge[side, 1, 0:radii],
            jedge[side, 0, 1:radii + 1], jedge[side, 1, 1:radii + 1], pa, pb)
        rows_w[side, 0], rows_w[side, 1] = ja, jb
        edge_sources.append(source)
        at = side * (cols - 1)
        sum_b[at:at + 1] = jnp.sum(source, axis=0, keepdims=True)

    def pieces(stage, own, part, tot, slots):
        half = own.shape[0] // 2
        mine = pl.ds(pl.multiple_of(core * half, 8), half)
        first = remote(own, part, part_send, part_recv.at[stage], partner, patch)
        sends = []
        for d in range(1, chips):
            if stage == 0:
                sends.append([
                    remote(tot.at[mine], slots.at[d - 1, mine], send_sem.at[d - 1, e],
                           recv_sem.at[d - 1, core], (chip + d) * 2 + e, patch)
                    for e in range(2)])
            else:
                sends.append([
                    remote(tot.at[mine], slots.at[d - 1, mine], send_sem.at[d - 1, 0],
                           recv_sem.at[d - 1, 1 + stage], (chip + d) * 2 + core, patch)])
        return mine, half, first, sends

    def forward(stage, pre, mine):
        return remote(pre.at[mine], pre.at[mine], fwd_send, fwd_recv.at[stage - 1], partner, patch)

    def rim_pieces(stage, rim, rtot, rpart, rslot):
        over = left * (1 - core) + right * core
        near = [
            remote(rim.at[0], rpart.at[1], rpart_send.at[0], rpart_recv.at[stage, 1], partner, left),
            remote(rim.at[1], rpart.at[0], rpart_send.at[1], rpart_recv.at[stage, 0], partner, right)]
        far = [[
            remote(rtot.at[core], rslot.at[d - 1, 1 - core], rim_send.at[d - 1, e],
                   rim_recv.at[stage, d - 1, 1 - core], (chip + d) * 2 + e, over)
            for e in range(2)] for d in range(1, chips)]
        return near, far

    def begin(stage, own, part, tot, slots, during, rims=None, lines=None):
        mine, half, first, sends = pieces(stage, own, part, tot, slots)
        first.start()
        if rims is not None:
            rim, rtot, rpart, rslot = rims
            for side in range(2):
                for i, r in enumerate(lines[side]):
                    rim[side, i:i + 1] = own[r:r + 1]
            near, far = rim_pieces(stage, rim, rtot, rpart, rslot)

            @pl.when(core == 0)
            def _():
                for copy in near:
                    copy.start()

        during()
        first.wait_recv()
        tot[mine] = own[mine] + part[mine]
        if rims is not None:
            for side in range(2):
                for i, r in enumerate(lines[side]):
                    rtot[side, i:i + 1] = own[r:r + 1] + part[r:r + 1]
        for d in range(chips - 1, 0, -1):
            @pl.when(chip + d < chips)
            def _():
                for copy in sends[d - 1]:
                    copy.start()
                if rims is not None:
                    for copy in far[d - 1]:
                        copy.start()

    def end(stage, own, part, tot, slots, out, rims=None, pre=None):
        mine, half, first, sends = pieces(stage, own, part, tot, slots)
        if rims is not None:
            rim, rtot, rpart, rslot = rims
            near, far = rim_pieces(stage, rim, rtot, rpart, rslot)

        @pl.when(core == 0)
        def _():
            out[...] = jnp.zeros_like(out)

        @pl.when(core == 1)
        def _():
            out[...] = part[...]
            if rims is not None:
                for copy in near:
                    copy.wait_recv()

        if rims is not None:
            @pl.when(core == 0)
            def _():
                rpart[...] = jnp.zeros_like(rpart)

        if stage == 0:
            for d in range(1, chips):
                @pl.when(chip >= d)
                def _():
                    for e in range(2):
                        piece = pl.ds(e * half, half)
                        remote(tot.at[piece], slots.at[d - 1, piece], send_sem.at[d - 1, e],
                               recv_sem.at[d - 1, e], shell, patch).wait_recv()
                    out[...] += slots[d - 1]
        else:
            @pl.when(chip > 0)
            def _():
                pre[mine] = jnp.zeros((half, lanes), f32)

            for d in range(1, chips):
                @pl.when(chip >= d)
                def _():
                    for copy in sends[d - 1]:
                        copy.wait_recv()
                    pre[mine] += slots[d - 1, mine]

            @pl.when(chip > 0)
            def _():
                fwd = forward(stage, pre, mine)
                fwd.start()
                fwd.wait_recv()
                out[...] += pre[...]

        if rims is not None:
            for d in range(1, chips):
                @pl.when(chip >= d)
                def _():
                    for e in range(2):
                        remote(rtot.at[e], rslot.at[d - 1, e], rim_send.at[d - 1, 0],
                               rim_recv.at[stage, d - 1, e], shell, patch).wait_recv()
                    rpart[...] += rslot[d - 1]

    def finish(stage, own, part, tot, slots, rims=None, pre=None):
        mine, half, first, sends = pieces(stage, own, part, tot, slots)
        first.wait_send()
        if rims is not None:
            near, far = rim_pieces(stage, *rims)

            @pl.when(core == 0)
            def _():
                for copy in near:
                    copy.wait_send()

        for d in range(1, chips):
            @pl.when(chip + d < chips)
            def _():
                for copy in sends[d - 1]:
                    copy.wait_send()
                if rims is not None:
                    for copy in far[d - 1]:
                        copy.wait_send()

        if stage > 0:
            @pl.when(chip > 0)
            def _():
                forward(stage, pre, mine).wait_send()

    if chips > 2:
        chain(chip == 0)
    pl.semaphore_wait(side_ready, 1)
    b_left = remote(bedge.at[0], bhalo.at[1], jh_send.at[0], edge_recv.at[1], shell, left)
    b_right = remote(bedge.at[1], bhalo.at[0], jh_send.at[1], edge_recv.at[0], shell, right)

    def finish_edges():
        row = lax.broadcasted_iota(jnp.int32, (radii, lanes), 0)
        for side in range(2):
            x, shift = edge_sources[side], 1
            while shift < radii:
                x = x + jnp.where(row >= shift, pltpu.roll(x, shift, 0), 0.0)
                shift *= 2
            bedge[side, side] = x
        b_left.start()
        b_right.start()

        def place(k, c):
            for side in range(2):
                at = side * (cols - 1)
                bp[k, PAD + at:PAD + at + 1, :] = bedge[side, side, pl.ds(k, 1), :]
                for f in range(2):
                    barj[f, k, at:at + 1, :] = rows_w[side, f, pl.ds(k, 1), :]
            for f in range(2):
                jp[f, k, before, :] = jhalo[0, f, pl.ds(k, 1), :]
                jp[f, k, after, :] = jhalo[1, f, pl.ds(k, 1), :]
            return c

        lax.fori_loop(0, radii, place, 0, unroll=4)

    rims_b = (rim_b, rtot_b, rpart_b, rslot_b)
    begin(0, sum_b, part_b, tot_b, slot_b, finish_edges, rims_b, ((0, 1), (cols - 2, cols - 1)))

    def local_step(k, carry):
        se, sa, sb, sja, sjb = carry
        beta = bp[k, inner]
        grow = jnp.exp((2.0 * step) * beta)
        es[k, inner] = grow
        dr[k, inner] = theta(beta)
        a, b = jp[0, k, inner], jp[1, k, inner]
        return (se + grow, sa + a, sb + b, sja + barj[0, k], sjb + barj[1, k])

    se, sa, sb, sja, sjb = lax.fori_loop(0, radii, local_step, (zero,) * 5, unroll=2)
    b_left.wait_recv()
    b_right.wait_recv()

    for side in range(2):
        x = bhalo[side, 1 - side]
        rows_w[side, 0] = jnp.exp((2.0 * step) * x)
        rows_w[side, 1] = theta(x)

    def halo_step(k, c):
        for i in range(2):
            bp[k, PAD - 2 + i:PAD - 1 + i, :] = bhalo[0, i, pl.ds(k, 1), :]
            bp[k, PAD + cols + i:PAD + cols + i + 1, :] = bhalo[1, i, pl.ds(k, 1), :]
        for side, at in enumerate((before, after)):
            es[k, at, :] = rows_w[side, 0, pl.ds(k, 1), :]
            dr[k, at, :] = rows_w[side, 1, pl.ds(k, 1), :]
        return c

    lax.fori_loop(0, radii, halo_step, 0, unroll=4)
    bt[...] = jnp.zeros_like(bt)
    end(0, sum_b, part_b, tot_b, slot_b, below_b, rims_b)
    finish(0, sum_b, part_b, tot_b, slot_b, rims_b)
    bt[inner] = below_b[...]
    bt[PAD - 2:PAD] = rpart_b[0]
    bt[PAD + cols:PAD + cols + 2] = rpart_b[1]

    first = PAD - 1
    mid, hi, lo = slice(first, first + tall), slice(first + 1, first + tall + 1), slice(first - 1, first + tall - 1)
    base_r = theta(bt[mid])
    base_i = bt[hi] - bt[lo]
    base_g = step * jnp.exp((2.0 * step) * bt[mid])
    wide_zero = jnp.zeros((tall, lanes), f32)

    def u_step(k, carry):
        ua, ub = carry
        growth = base_g * es[k, mid]
        br = dr[k, mid] + base_r
        bi = 0.5 * ((bp[k, hi] - bp[k, lo]) + base_i)
        a, b = jp[0, k, mid], jp[1, k, mid]
        ua = ua + growth * (br - (a * br + b * bi))
        ub = ub + growth * (bi - (b * br - a * bi))
        up[0, k, mid] = ua
        up[1, k, mid] = ub
        return ua, ub

    ua_sum, ub_sum = lax.fori_loop(0, radii, u_step, (wide_zero, wide_zero), unroll=2)
    sum_u[:cols] = ua_sum[1:cols + 1]
    sum_u[cols:] = ub_sum[1:cols + 1]
    full_b = bt[inner]
    grow_b = jnp.exp((2.0 * step) * full_b)

    def wh_step(k, carry):
        sw, ha, hb = carry
        beta = bp[k, inner] + full_b
        growth = grow_b * es[k, inner]
        a, b = jp[0, k, inner], jp[1, k, inner]
        ua, ub = up[0, k, inner], up[1, k, inner]
        ta, tb = theta(ua), theta(ub)
        pa = 0.5 * (up[0, k, above] - up[0, k, below])
        pb = 0.5 * (up[1, k, above] - up[1, k, below])
        ja, jb = barj[0, k], barj[1, k]
        sw = sw + (growth * (ta + pb) + (b * ua - a * ub))
        ha = ha + ((ta - pb) + ua * ja - ub * jb + beta * a)
        hb = hb + ((tb + pa) + ua * jb + ub * ja + beta * b)
        cw[k] = sw
        ch[0, k] = ha
        ch[1, k] = hb
        return sw, ha, hb

    done = []
    ahead = radii // 4
    rims_u = (rim_u, rtot_u, rpart_u, rslot_u)
    begin(1, sum_u, part_u, tot_u, slot_u,
          lambda: done.extend(lax.fori_loop(0, ahead, wh_step, (zero, zero, zero))),
          rims_u, ((0, cols), (cols - 1, 2 * cols - 1)))
    sw, ha, hb = lax.fori_loop(ahead, radii, wh_step, tuple(done))
    end(1, sum_u, part_u, tot_u, slot_u, below_u, rims_u, pre_u)
    finish(1, sum_u, part_u, tot_u, slot_u, rims_u, pre_u)
    for f in range(2):
        ct[f] = jnp.zeros(ct.shape[1:], f32)
        ct[f, inner] = below_u[f * cols:(f + 1) * cols]
        ct[f, PAD - 1:PAD] = rpart_u[0, f:f + 1]
        ct[f, PAD + cols:PAD + cols + 1] = rpart_u[1, f:f + 1]
    ca, cb = ct[0, inner], ct[1, inner]
    re_bar, eth_a, eth_b = eth_planes(theta, ct, inner, above, below)
    n = float(radii)
    sum_h[:cols] = sw + (grow_b * se) * re_bar + (sb * ca - sa * cb)
    sum_h[cols:2 * cols] = ha + n * eth_a + (ca * sja - cb * sjb)
    sum_h[2 * cols:] = hb + n * eth_b + (ca * sjb + cb * sja)

    def fields_step(k, carry):
        dw, da, db = carry
        a, b = jp[0, k, inner], jp[1, k, inner]
        ja, jb = barj[0, k], barj[1, k]
        dw = dw + ((grow_b * es[k, inner]) * re_bar + (b * ca - a * cb))
        da = da + (eth_a + (ca * ja - cb * jb))
        db = db + (eth_b + (ca * jb + cb * ja))
        bfin[k] = step * (bp[k, inner] + full_b)
        ufin[0, k] = step * (up[0, k, inner] + ca)
        ufin[1, k] = step * (up[1, k, inner] + cb)
        cw[k] = cw[k] + dw
        ch[0, k] = ch[0, k] + da
        ch[1, k] = ch[1, k] + db
        return dw, da, db

    begin(2, sum_h, part_h, tot_h, slot_h, lambda: None)
    lax.fori_loop(0, radii, fields_step, (zero, zero, zero), unroll=2)
    end(2, sum_h, part_h, tot_h, slot_h, below_h, None, pre_h)

    @pl.when(shell > 0)
    def _():
        down(shell - 1).wait_send()

    b_left.wait_send()
    b_right.wait_send()
    finish(2, sum_h, part_h, tot_h, slot_h, None, pre_h)


def tail(step, bfin, ufin, cw, ch, below_h, beta_out, u_out, w_out, h_out, wv, hv, first_sems, sems):
    radii, cols, _ = cw.shape
    copies = [pltpu.make_async_copy(bfin, beta_out, first_sems.at[0]),
              pltpu.make_async_copy(ufin, u_out, first_sems.at[1])]
    for copy in copies:
        copy.start()
    w, ha, hb = (below_h[i * cols:(i + 1) * cols] for i in range(3))
    sq = step * step

    def final(k, c):
        wv[k] = sq * (cw[k] + w)
        hv[0, k] = sq * (ch[0, k] + ha)
        hv[1, k] = sq * (ch[1, k] + hb)
        return c

    chunks = sems.shape[0]
    size = radii // chunks
    for i in range(chunks):
        lax.fori_loop(i * size, (i + 1) * size, final, 0, unroll=4)
        at = pl.ds(i * size, size)
        more = [pltpu.make_async_copy(wv.at[at], w_out.at[at], sems.at[i, 0]),
                pltpu.make_async_copy(hv.at[:, at], h_out.at[:, at], sems.at[i, 1])]
        for copy in more:
            copy.start()
        copies += more
    for copy in copies:
        copy.wait()


def solution(mesh):
    shells, patches = mesh.shape["shell"], mesh.shape["patch"]
    chips = shells // 2

    def local(field_j):
        _, radii, cols, lanes = field_j.shape
        step = 1.0 / math.sqrt(radii * shells)
        f32 = jnp.float32
        vm = lambda *s: pltpu.VMEM(s, f32)
        shape = lambda *s: jax.ShapeDtypeStruct(s, f32)
        tall = cols + 2 * PAD
        dma = pltpu.SemaphoreType.DMA
        vmem = pl.BlockSpec(memory_space=pltpu.VMEM)
        hbm = pl.BlockSpec(memory_space=pltpu.HBM)
        plain, pair = (radii, cols, lanes), (2, radii, cols, lanes)
        padded = (2, radii, tall, lanes)
        limit = 24 * 1024 * 1024
        many = max(chips - 1, 1)
        regular = pltpu.SemaphoreType.REGULAR
        planes = vm(2, 2, radii, lanes)
        scratch = [vm(*padded), vm(*pair), vm(*padded), vm(2, tall, lanes)]
        scratch += [vm(radii, tall, lanes)] * 3 + [vm(tall, lanes), planes, planes, vm(cols, lanes), vm(2 * cols, lanes),
                                                  vm(2, cols, lanes), vm(2, 2, radii + 8, lanes), planes, planes, planes]
        for n in (1, 2, 3):
            scratch += [vm(n * cols, lanes)] * 3 + [vm(many, n * cols, lanes)] + [vm(n * cols, lanes)] * (n > 1)
        for _ in range(2):
            scratch += [vm(2, 2, lanes)] * 3 + [vm(many, 2, 2, lanes)]
        scratch += [dma, dma((2,)), dma((2,)), dma((2,)), regular, regular, regular,
                    dma((2,)), dma, dma((3,)), dma((many, 2)), dma((many, 4)), dma, dma((2,)),
                    dma((2,)), dma((2, 2)), dma((many, 2)), dma((2, many, 2))]
        found = pl.pallas_call(
            functools.partial(kernel, shells, patches, step),
            out_shape=(shape(*plain), shape(*pair), shape(*plain), shape(*pair), shape(3 * cols, lanes)),
            in_specs=[hbm],
            out_specs=(vmem,) * 5,
            scratch_shapes=scratch,
            compiler_params=pltpu.CompilerParams(
                collective_id=0, has_side_effects=True, vmem_limit_bytes=limit),
        )(pltpu.with_memory_space_constraint(field_j, pltpu.HBM))
        return pl.pallas_call(
            functools.partial(tail, step),
            out_shape=(shape(*plain), shape(*pair), shape(*plain), shape(*pair)),
            in_specs=[vmem] * 5,
            out_specs=(hbm,) * 4,
            scratch_shapes=[vm(*plain), vm(*pair), dma((2,)), dma((2, 2))],
            compiler_params=pltpu.CompilerParams(vmem_limit_bytes=limit),
        )(*found)

    return jax.shard_map(
        local,
        mesh=mesh,
        in_specs=(P(None, "shell", "patch", None),),
        out_specs=(
            P("shell", "patch", None),
            P(None, "shell", "patch", None),
            P("shell", "patch", None),
            P(None, "shell", "patch", None),
        ),
        check_vma=False,
    )
```

```python
import functools
import math

import jax
import jax.numpy as jnp
from jax import lax
from jax.experimental import pallas as pl
from jax.experimental.pallas import tpu as pltpu
from jax.sharding import PartitionSpec as P

PAD = 8


def remote(src, dst, send_sem, recv_sem, shell, patch):
    return pltpu.make_async_remote_copy(
        src_ref=src,
        dst_ref=dst,
        send_sem=send_sem,
        recv_sem=recv_sem,
        device_id=(shell, patch),
        device_id_type=pl.DeviceIdType.MESH,
    )


def make_theta(lanes):
    lane = lax.broadcasted_iota(jnp.int32, (8, lanes), 1)
    keep_f = jnp.where(lane == lanes - 1, 0.0, 0.5).astype(jnp.float32)
    keep_b = jnp.where(lane == 0, 0.0, 0.5).astype(jnp.float32)

    def theta(x):
        reps = x.shape[0] // 8
        mf = jnp.concatenate([keep_f] * reps, axis=0) if reps > 1 else keep_f
        mb = jnp.concatenate([keep_b] * reps, axis=0) if reps > 1 else keep_b
        return pltpu.roll(x, lanes - 1, 1) * mf - pltpu.roll(x, 1, 1) * mb

    return theta


def eth_planes(theta, pair, inner, above, below):
    ta, tb = theta(pair[0, inner]), theta(pair[1, inner])
    pa = 0.5 * (pair[0, above] - pair[0, below])
    pb = 0.5 * (pair[1, above] - pair[1, below])
    return ta + pb, ta - pb, tb + pa


def beta_terms(theta, a, b, next_a, next_b, pa, pb):
    ra, rb = next_a - a, next_b - b
    ta, tb = theta(a), theta(b)
    ea, eb = ta - pb, tb + pa
    return 0.25 * (0.5 * (ra * ra + rb * rb) - (ea * ea + eb * eb)), ta + pb, tb - pa


def kernel(shells, patches, step, j_hbm, bfin, ufin, cw, ch, below_h,
           jp, barj, up, ct, bp, es, dr, bt, bedge, bhalo, below_b, below_u, jnext, jedge, jside, jhalo, rows_w,
           sum_b, part_b, tot_b, slot_b,
           sum_u, part_u, tot_u, slot_u, pre_u,
           sum_h, part_h, tot_h, slot_h, pre_h,
           rim_b, rtot_b, rpart_b, rslot_b, rim_u, rtot_u, rpart_u, rslot_u,
           load_sem, rad_sem, jh_send, jh_recv, next_ready, up_ready, side_ready,
           edge_recv, part_send, part_recv, send_sem, recv_sem, fwd_send, fwd_recv,
           rpart_send, rpart_recv, rim_send, rim_recv):
    radii, cols, lanes = cw.shape
    tall = cols + 8
    f32 = jnp.float32
    chips = shells // 2
    shell, patch = lax.axis_index("shell"), lax.axis_index("patch")
    chip, core = shell // 2, shell % 2
    partner = shell + 1 - 2 * core
    right = lax.rem(patch + 1, patches)
    left = lax.rem(patch + patches - 1, patches)
    inner = slice(PAD, PAD + cols)
    above = slice(PAD + 1, PAD + cols + 1)
    below = slice(PAD - 1, PAD + cols - 1)
    before, after = slice(PAD - 1, PAD), slice(PAD + cols, PAD + cols + 1)
    theta = make_theta(lanes)
    mesh_id = pl.DeviceIdType.MESH

    load = pltpu.make_async_copy(j_hbm, jp.at[:, :, pl.ds(PAD, cols), :], load_sem)
    load.start()

    barrier = pltpu.get_barrier_semaphore()
    def greet(there, p):
        pl.semaphore_signal(barrier, inc=1, device_id=(there, p), device_id_type=mesh_id)

    greet(partner, patch)
    greet(shell, left)
    greet(shell, right)

    @pl.when(chip < chips - 1)
    def _():
        greet(shell + 2, patch)

        @pl.when(chip < chips - 2)
        def _():
            greet(shell + 4, patch)

        @pl.when(core == 1)
        def _():
            greet(shell + 1, patch)

    load.wait()

    def pack(k, c):
        for f in range(2):
            jedge[0, f, pl.ds(k, 1), :] = jp[f, k, PAD:PAD + 1, :]
            jedge[1, f, pl.ds(k, 1), :] = jp[f, k, PAD + cols - 1:PAD + cols, :]
        return c

    lax.fori_loop(0, radii, pack, 0, unroll=8)
    inside, second = (chip > 0).astype(jnp.int32), (chip > 1).astype(jnp.int32)
    pl.semaphore_wait(barrier, 3 + inside * (2 - core) + second)
    to_left = remote(jedge.at[0, :, pl.ds(0, radii)], jhalo.at[1], jh_send.at[0], jh_recv.at[1], shell, left)
    to_right = remote(jedge.at[1, :, pl.ds(0, radii)], jhalo.at[0], jh_send.at[1], jh_recv.at[0], shell, right)
    to_left.start()
    to_right.start()

    @pl.when(chip > 0)
    def _():
        pl.semaphore_signal(next_ready, inc=1, device_id=(shell - 2, patch), device_id_type=mesh_id)

    def chain(step_at):
        @pl.when(step_at)
        def _():
            @pl.when(chip < chips - 1)
            def _():
                pl.semaphore_wait(next_ready, 1)

            @pl.when(chip < chips - 2)
            def _():
                pl.semaphore_wait(up_ready, 1)

            @pl.when(chip > 1)
            def _():
                pl.semaphore_signal(up_ready, inc=1, device_id=(shell - 4, patch), device_id_type=mesh_id)

            pl.semaphore_signal(side_ready, inc=1, device_id=(partner, patch), device_id_type=mesh_id)

    chain(chip == chips - 1)

    def down(there):
        return remote(j_hbm.at[:, 0], jnext, rad_sem.at[0], rad_sem.at[1], there, patch)

    @pl.when(shell > 0)
    def _():
        down(shell - 1).start()

    def pack_side(k, c):
        for f in range(2):
            jside[0, f, pl.ds(k, 1), :] = jp[f, k, PAD + 1:PAD + 2, :]
            jside[1, f, pl.ds(k, 1), :] = jp[f, k, PAD + cols - 2:PAD + cols - 1, :]
        return c

    lax.fori_loop(0, radii, pack_side, 0, unroll=8)

    def beta_step(k, next_a, next_b, total):
        pa = 0.5 * (jp[0, k, above] - jp[0, k, below])
        pb = 0.5 * (jp[1, k, above] - jp[1, k, below])
        source, ja, jb = beta_terms(theta, jp[0, k, inner], jp[1, k, inner], next_a, next_b, pa, pb)
        barj[0, k], barj[1, k] = ja, jb
        total = total + source
        bp[k, inner] = total
        bedge[0, 1, pl.ds(k, 1), :] = total[1:2]
        bedge[1, 0, pl.ds(k, 1), :] = total[cols - 2:cols - 1]
        return total

    zero = jnp.zeros((cols, lanes), f32)
    total = zero
    slices = 4
    for i in range(slices):
        stop = (i + 1) * radii // slices if i < slices - 1 else radii - 1
        total = lax.fori_loop(
            i * radii // slices, stop,
            lambda k, t: beta_step(k, jp[0, k + 1, inner], jp[1, k + 1, inner], t), total, unroll=2)
        if i == slices // 2 - 1 and chips > 1:
            chain(chip == chips - 2)

    @pl.when(shell == shells - 1)
    def _():
        for f in range(2):
            jnext[f] = jp[f, radii - 1, inner]

    @pl.when(shell < shells - 1)
    def _():
        down(shell).wait_recv()

    sum_b[...] = beta_step(radii - 1, jnext[0], jnext[1], total)
    for f in range(2):
        jedge[0, f, radii:radii + 1] = jnext[f, 0:1]
        jedge[1, f, radii:radii + 1] = jnext[f, cols - 1:cols]
    for c in range(chips - 3, 0, -1):
        chain(chip == c)
    to_left.wait_recv()
    to_right.wait_recv()
    to_left.wait_send()
    to_right.wait_send()
    edge_sources = []
    for side, (over, under) in enumerate(((jside.at[0], jhalo.at[0]), (jhalo.at[1], jside.at[1]))):
        pa, pb = (0.5 * (over[f] - under[f]) for f in range(2))
        source, ja, jb = beta_terms(
            theta, jedge[side, 0, 0:radii], jedge[side, 1, 0:radii],
            jedge[side, 0, 1:radii + 1], jedge[side, 1, 1:radii + 1], pa, pb)
        rows_w[side, 0], rows_w[side, 1] = ja, jb
        edge_sources.append(source)
        at = side * (cols - 1)
        sum_b[at:at + 1] = jnp.sum(source, axis=0, keepdims=True)

    def pieces(stage, own, part, tot, slots):
        half = own.shape[0] // 2
        mine = pl.ds(pl.multiple_of(core * half, 8), half)
        first = remote(own, part, part_send, part_recv.at[stage], partner, patch)
        sends = []
        for d in range(1, chips):
            if stage == 0:
                sends.append([
                    remote(tot.at[mine], slots.at[d - 1, mine], send_sem.at[d - 1, e],
                           recv_sem.at[d - 1, core], (chip + d) * 2 + e, patch)
                    for e in range(2)])
            else:
                sends.append([
                    remote(tot.at[mine], slots.at[d - 1, mine], send_sem.at[d - 1, 0],
                           recv_sem.at[d - 1, 1 + stage], (chip + d) * 2 + core, patch)])
        return mine, half, first, sends

    def forward(stage, pre, mine):
        return remote(pre.at[mine], pre.at[mine], fwd_send, fwd_recv.at[stage - 1], partner, patch)

    def rim_pieces(stage, rim, rtot, rpart, rslot):
        over = left * (1 - core) + right * core
        near = [
            remote(rim.at[0], rpart.at[1], rpart_send.at[0], rpart_recv.at[stage, 1], partner, left),
            remote(rim.at[1], rpart.at[0], rpart_send.at[1], rpart_recv.at[stage, 0], partner, right)]
        far = [[
            remote(rtot.at[core], rslot.at[d - 1, 1 - core], rim_send.at[d - 1, e],
                   rim_recv.at[stage, d - 1, 1 - core], (chip + d) * 2 + e, over)
            for e in range(2)] for d in range(1, chips)]
        return near, far

    def begin(stage, own, part, tot, slots, during, rims=None, lines=None):
        mine, half, first, sends = pieces(stage, own, part, tot, slots)
        first.start()
        if rims is not None:
            rim, rtot, rpart, rslot = rims
            for side in range(2):
                for i, r in enumerate(lines[side]):
                    rim[side, i:i + 1] = own[r:r + 1]
            near, far = rim_pieces(stage, rim, rtot, rpart, rslot)

            @pl.when(core == 0)
            def _():
                for copy in near:
                    copy.start()

        during()
        first.wait_recv()
        tot[mine] = own[mine] + part[mine]
        if rims is not None:
            for side in range(2):
                for i, r in enumerate(lines[side]):
                    rtot[side, i:i + 1] = own[r:r + 1] + part[r:r + 1]
        for d in (range(1, chips) if stage in (1,) else range(chips - 1, 0, -1)):
            @pl.when(chip + d < chips)
            def _():
                for copy in sends[d - 1]:
                    copy.start()
                if rims is not None:
                    for copy in far[d - 1]:
                        copy.start()

    def end(stage, own, part, tot, slots, out, rims=None, pre=None):
        mine, half, first, sends = pieces(stage, own, part, tot, slots)
        if rims is not None:
            rim, rtot, rpart, rslot = rims
            near, far = rim_pieces(stage, rim, rtot, rpart, rslot)

        @pl.when(core == 0)
        def _():
            out[...] = jnp.zeros_like(out)

        @pl.when(core == 1)
        def _():
            out[...] = part[...]
            if rims is not None:
                for copy in near:
                    copy.wait_recv()

        if rims is not None:
            @pl.when(core == 0)
            def _():
                rpart[...] = jnp.zeros_like(rpart)

        if stage == 0:
            for d in range(1, chips):
                @pl.when(chip >= d)
                def _():
                    for e in range(2):
                        piece = pl.ds(e * half, half)
                        remote(tot.at[piece], slots.at[d - 1, piece], send_sem.at[d - 1, e],
                               recv_sem.at[d - 1, e], shell, patch).wait_recv()
                    out[...] += slots[d - 1]
        else:
            @pl.when(chip > 0)
            def _():
                pre[mine] = jnp.zeros((half, lanes), f32)

            for d in range(1, chips):
                @pl.when(chip >= d)
                def _():
                    for copy in sends[d - 1]:
                        copy.wait_recv()
                    pre[mine] += slots[d - 1, mine]

            @pl.when(chip > 0)
            def _():
                fwd = forward(stage, pre, mine)
                fwd.start()
                fwd.wait_recv()
                out[...] += pre[...]

        if rims is not None:
            for d in range(1, chips):
                @pl.when(chip >= d)
                def _():
                    for e in range(2):
                        remote(rtot.at[e], rslot.at[d - 1, e], rim_send.at[d - 1, 0],
                               rim_recv.at[stage, d - 1, e], shell, patch).wait_recv()
                    rpart[...] += rslot[d - 1]

    def finish(stage, own, part, tot, slots, rims=None, pre=None):
        mine, half, first, sends = pieces(stage, own, part, tot, slots)
        first.wait_send()
        if rims is not None:
            near, far = rim_pieces(stage, *rims)

            @pl.when(core == 0)
            def _():
                for copy in near:
                    copy.wait_send()

        for d in range(1, chips):
            @pl.when(chip + d < chips)
            def _():
                for copy in sends[d - 1]:
                    copy.wait_send()
                if rims is not None:
                    for copy in far[d - 1]:
                        copy.wait_send()

        if stage > 0:
            @pl.when(chip > 0)
            def _():
                forward(stage, pre, mine).wait_send()

    b_left = remote(bedge.at[0], bhalo.at[1], jh_send.at[0], edge_recv.at[1], shell, left)
    b_right = remote(bedge.at[1], bhalo.at[0], jh_send.at[1], edge_recv.at[0], shell, right)
    row = lax.broadcasted_iota(jnp.int32, (radii, lanes), 0)
    for side in range(2):
        x, shift = edge_sources[side], 1
        while shift < radii:
            x = x + jnp.where(row >= shift, pltpu.roll(x, shift, 0), 0.0)
            shift *= 2
        bedge[side, side] = x
    b_left.start()
    b_right.start()
    if chips > 2:
        chain(chip == 0)
    pl.semaphore_wait(side_ready, 1)
    def finish_edges():
        def place(k, c):
            for side in range(2):
                at = side * (cols - 1)
                bp[k, PAD + at:PAD + at + 1, :] = bedge[side, side, pl.ds(k, 1), :]
                for f in range(2):
                    barj[f, k, at:at + 1, :] = rows_w[side, f, pl.ds(k, 1), :]
            for f in range(2):
                jp[f, k, before, :] = jhalo[0, f, pl.ds(k, 1), :]
                jp[f, k, after, :] = jhalo[1, f, pl.ds(k, 1), :]
            return c

        lax.fori_loop(0, radii, place, 0, unroll=4)

    rims_b = (rim_b, rtot_b, rpart_b, rslot_b)
    begin(0, sum_b, part_b, tot_b, slot_b, finish_edges, rims_b, ((0, 1), (cols - 2, cols - 1)))

    def local_step(k, carry):
        se, sa, sb, sja, sjb = carry
        beta = bp[k, inner]
        grow = jnp.exp((2.0 * step) * beta)
        es[k, inner] = grow
        dr[k, inner] = theta(beta)
        a, b = jp[0, k, inner], jp[1, k, inner]
        return (se + grow, sa + a, sb + b, sja + barj[0, k], sjb + barj[1, k])

    se, sa, sb, sja, sjb = lax.fori_loop(0, radii, local_step, (zero,) * 5, unroll=2)
    b_left.wait_recv()
    b_right.wait_recv()

    for side in range(2):
        x = bhalo[side, 1 - side]
        rows_w[side, 0] = jnp.exp((2.0 * step) * x)
        rows_w[side, 1] = theta(x)

    def halo_step(k, c):
        for i in range(2):
            bp[k, PAD - 2 + i:PAD - 1 + i, :] = bhalo[0, i, pl.ds(k, 1), :]
            bp[k, PAD + cols + i:PAD + cols + i + 1, :] = bhalo[1, i, pl.ds(k, 1), :]
        for side, at in enumerate((before, after)):
            es[k, at, :] = rows_w[side, 0, pl.ds(k, 1), :]
            dr[k, at, :] = rows_w[side, 1, pl.ds(k, 1), :]
        return c

    lax.fori_loop(0, radii, halo_step, 0, unroll=4)
    bt[...] = jnp.zeros_like(bt)
    end(0, sum_b, part_b, tot_b, slot_b, below_b, rims_b)
    finish(0, sum_b, part_b, tot_b, slot_b, rims_b)
    bt[inner] = below_b[...]
    bt[PAD - 2:PAD] = rpart_b[0]
    bt[PAD + cols:PAD + cols + 2] = rpart_b[1]

    first = PAD - 1
    mid, hi, lo = slice(first, first + tall), slice(first + 1, first + tall + 1), slice(first - 1, first + tall - 1)
    base_r = theta(bt[mid])
    base_i = bt[hi] - bt[lo]
    base_g = step * jnp.exp((2.0 * step) * bt[mid])
    wide_zero = jnp.zeros((tall, lanes), f32)

    def u_step(k, carry):
        ua, ub = carry
        growth = base_g * es[k, mid]
        br = dr[k, mid] + base_r
        bi = 0.5 * ((bp[k, hi] - bp[k, lo]) + base_i)
        a, b = jp[0, k, mid], jp[1, k, mid]
        ua = ua + growth * (br - (a * br + b * bi))
        ub = ub + growth * (bi - (b * br - a * bi))
        up[0, k, mid] = ua
        up[1, k, mid] = ub
        return ua, ub

    ua_sum, ub_sum = lax.fori_loop(0, radii, u_step, (wide_zero, wide_zero), unroll=2)
    sum_u[:cols] = ua_sum[1:cols + 1]
    sum_u[cols:] = ub_sum[1:cols + 1]
    full_b = bt[inner]
    grow_b = jnp.exp((2.0 * step) * full_b)

    def wh_step(k, carry):
        sw, ha, hb = carry
        beta = bp[k, inner] + full_b
        growth = grow_b * es[k, inner]
        a, b = jp[0, k, inner], jp[1, k, inner]
        ua, ub = up[0, k, inner], up[1, k, inner]
        ta, tb = theta(ua), theta(ub)
        pa = 0.5 * (up[0, k, above] - up[0, k, below])
        pb = 0.5 * (up[1, k, above] - up[1, k, below])
        ja, jb = barj[0, k], barj[1, k]
        sw = sw + (growth * (ta + pb) + (b * ua - a * ub))
        ha = ha + ((ta - pb) + ua * ja - ub * jb + beta * a)
        hb = hb + ((tb + pa) + ua * jb + ub * ja + beta * b)
        cw[k] = sw
        ch[0, k] = ha
        ch[1, k] = hb
        return sw, ha, hb

    done = []
    ahead = radii // 4
    rims_u = (rim_u, rtot_u, rpart_u, rslot_u)
    begin(1, sum_u, part_u, tot_u, slot_u,
          lambda: done.extend(lax.fori_loop(0, ahead, wh_step, (zero, zero, zero))),
          rims_u, ((0, cols), (cols - 1, 2 * cols - 1)))
    sw, ha, hb = lax.fori_loop(ahead, radii, wh_step, tuple(done))
    end(1, sum_u, part_u, tot_u, slot_u, below_u, rims_u, pre_u)
    finish(1, sum_u, part_u, tot_u, slot_u, rims_u, pre_u)
    for f in range(2):
        ct[f] = jnp.zeros(ct.shape[1:], f32)
        ct[f, inner] = below_u[f * cols:(f + 1) * cols]
        ct[f, PAD - 1:PAD] = rpart_u[0, f:f + 1]
        ct[f, PAD + cols:PAD + cols + 1] = rpart_u[1, f:f + 1]
    ca, cb = ct[0, inner], ct[1, inner]
    re_bar, eth_a, eth_b = eth_planes(theta, ct, inner, above, below)
    n = float(radii)
    sum_h[:cols] = sw + (grow_b * se) * re_bar + (sb * ca - sa * cb)
    sum_h[cols:2 * cols] = ha + n * eth_a + (ca * sja - cb * sjb)
    sum_h[2 * cols:] = hb + n * eth_b + (ca * sjb + cb * sja)

    def fields_step(k, carry):
        dw, da, db = carry
        a, b = jp[0, k, inner], jp[1, k, inner]
        ja, jb = barj[0, k], barj[1, k]
        dw = dw + ((grow_b * es[k, inner]) * re_bar + (b * ca - a * cb))
        da = da + (eth_a + (ca * ja - cb * jb))
        db = db + (eth_b + (ca * jb + cb * ja))
        bfin[k] = step * (bp[k, inner] + full_b)
        ufin[0, k] = step * (up[0, k, inner] + ca)
        ufin[1, k] = step * (up[1, k, inner] + cb)
        cw[k] = cw[k] + dw
        ch[0, k] = ch[0, k] + da
        ch[1, k] = ch[1, k] + db
        return dw, da, db

    begin(2, sum_h, part_h, tot_h, slot_h, lambda: None)
    lax.fori_loop(0, radii, fields_step, (zero, zero, zero), unroll=2)
    end(2, sum_h, part_h, tot_h, slot_h, below_h, None, pre_h)

    @pl.when(shell > 0)
    def _():
        down(shell - 1).wait_send()

    b_left.wait_send()
    b_right.wait_send()
    finish(2, sum_h, part_h, tot_h, slot_h, None, pre_h)


def tail(step, bfin, ufin, cw, ch, below_h, beta_out, u_out, w_out, h_out, wv, hv, first_sems, sems):
    radii, cols, _ = cw.shape
    copies = [pltpu.make_async_copy(bfin, beta_out, first_sems.at[0]),
              pltpu.make_async_copy(ufin, u_out, first_sems.at[1])]
    for copy in copies:
        copy.start()
    w, ha, hb = (below_h[i * cols:(i + 1) * cols] for i in range(3))
    sq = step * step

    def final(k, c):
        wv[k] = sq * (cw[k] + w)
        hv[0, k] = sq * (ch[0, k] + ha)
        hv[1, k] = sq * (ch[1, k] + hb)
        return c

    chunks = sems.shape[0]
    size = radii // chunks
    for i in range(chunks):
        lax.fori_loop(i * size, (i + 1) * size, final, 0, unroll=4)
        at = pl.ds(i * size, size)
        more = [pltpu.make_async_copy(wv.at[at], w_out.at[at], sems.at[i, 0]),
                pltpu.make_async_copy(hv.at[:, at], h_out.at[:, at], sems.at[i, 1])]
        for copy in more:
            copy.start()
        copies += more
    for copy in copies:
        copy.wait()


def solution(mesh):
    shells, patches = mesh.shape["shell"], mesh.shape["patch"]
    chips = shells // 2

    def local(field_j):
        _, radii, cols, lanes = field_j.shape
        step = 1.0 / math.sqrt(radii * shells)
        f32 = jnp.float32
        vm = lambda *s: pltpu.VMEM(s, f32)
        shape = lambda *s: jax.ShapeDtypeStruct(s, f32)
        tall = cols + 2 * PAD
        dma = pltpu.SemaphoreType.DMA
        vmem = pl.BlockSpec(memory_space=pltpu.VMEM)
        hbm = pl.BlockSpec(memory_space=pltpu.HBM)
        plain, pair = (radii, cols, lanes), (2, radii, cols, lanes)
        padded = (2, radii, tall, lanes)
        limit = 24 * 1024 * 1024
        many = max(chips - 1, 1)
        regular = pltpu.SemaphoreType.REGULAR
        planes = vm(2, 2, radii, lanes)
        scratch = [vm(*padded), vm(*pair), vm(*padded), vm(2, tall, lanes)]
        scratch += [vm(radii, tall, lanes)] * 3 + [vm(tall, lanes), planes, planes, vm(cols, lanes), vm(2 * cols, lanes),
                                                  vm(2, cols, lanes), vm(2, 2, radii + 8, lanes), planes, planes, planes]
        for n in (1, 2, 3):
            scratch += [vm(n * cols, lanes)] * 3 + [vm(many, n * cols, lanes)] + [vm(n * cols, lanes)] * (n > 1)
        for _ in range(2):
            scratch += [vm(2, 2, lanes)] * 3 + [vm(many, 2, 2, lanes)]
        scratch += [dma, dma((2,)), dma((2,)), dma((2,)), regular, regular, regular,
                    dma((2,)), dma, dma((3,)), dma((many, 2)), dma((many, 4)), dma, dma((2,)),
                    dma((2,)), dma((2, 2)), dma((many, 2)), dma((2, many, 2))]
        found = pl.pallas_call(
            functools.partial(kernel, shells, patches, step),
            out_shape=(shape(*plain), shape(*pair), shape(*plain), shape(*pair), shape(3 * cols, lanes)),
            in_specs=[hbm],
            out_specs=(vmem,) * 5,
            scratch_shapes=scratch,
            compiler_params=pltpu.CompilerParams(
                collective_id=0, has_side_effects=True, vmem_limit_bytes=limit),
        )(pltpu.with_memory_space_constraint(field_j, pltpu.HBM))
        return pl.pallas_call(
            functools.partial(tail, step),
            out_shape=(shape(*plain), shape(*pair), shape(*plain), shape(*pair)),
            in_specs=[vmem] * 5,
            out_specs=(hbm,) * 4,
            scratch_shapes=[vm(*plain), vm(*pair), dma((2,)), dma((2, 2))],
            compiler_params=pltpu.CompilerParams(vmem_limit_bytes=limit),
        )(*found)

    return jax.shard_map(
        local,
        mesh=mesh,
        in_specs=(P(None, "shell", "patch", None),),
        out_specs=(
            P("shell", "patch", None),
            P(None, "shell", "patch", None),
            P("shell", "patch", None),
            P(None, "shell", "patch", None),
        ),
        check_vma=False,
    )
```
